256 devices in a mesh: seq: 64 (over z, y, core), exp: 4 (over x).
Axes of the slice: x: 4, y: 4, z: 8, core: 2. Of those that a mesh axis runs over, the one named last changes fastest.
Arguments:
- query_in: bfloat16 [32768, 2048], P('seq', 'exp'), may hold values from -0.52734375 to 0.52734375
- key_in: bfloat16 [32768, 2048], P('seq', 'exp'), may hold values from -0.52734375 to 0.52734375
- value_in: bfloat16 [32768, 2048], P('seq', 'exp'), may hold values from -0.52734375 to 0.52734375
- out_grad: bfloat16 [32768, 2048], P('seq', 'exp'), may hold values from -0.375 to 0.375
- inputs: bfloat16 [32768, 1024], P('seq'), may hold values from -0.125 to 0.125
- expert_ids: int32 [32768, 2], P('seq'), may hold values from 0 to 3, all different within a row; in each aligned block of 512 rows (0 to 511, 512 to 1023, ...) at most 384 rows name the same one
- route_gates: float32 [32768, 2], P('seq'), may hold values from 0.2 to 1
- expert_weight: bfloat16 [4, 1024, 4096], P('exp'), may hold values from -0.09375 to 0.09375
Outputs:
- gradient_of_queries: bfloat16 [32768, 2048], P('seq', 'exp')
- gradient_of_keys: bfloat16 [32768, 2048], P('seq', 'exp')
- value_grad: bfloat16 [32768, 2048], P('seq', 'exp')
- input_grad: bfloat16 [32768, 1024], P('seq', 'exp')
- weight_grad: float32 [4, 1024, 4096], P('exp', 'seq')
The draws below stay inside these ranges and needn't reach their ends.
Inputs may be any that keep to these rules, and one draw needn't show every extreme that they name: `expert_ids`: each token names two different experts. Among the 512 tokens of one index of seq no expert is named more than 384 times, a bound that some block reaches in some of them.
All inputs are finite; a program needn't handle non-finite values.
Results may differ from the reference program's by a relative error of at most 0.013.
Values may be sent and summed in bfloat16 or wider, within the bound.
A program may use at most 128 MiB of HBM per device.

```python
import math
import jax
import jax.numpy as jnp
import numpy as np
from jax import lax

HEADS = 16
DH = 128
DIN = 1024
TOK_DEV = 512
TOKENS = 32768
EXPERTS = 4
CAP = 384
N_SEQ = 64


def with_spikes(values, key, source, target, blocks, factor):
    owner, partner = [(jnp.arange(values.shape[dim]) // (values.shape[dim] // blocks)).reshape([-1 if axis == dim else 1 for axis in range(values.ndim)]) for dim in (source, target)]
    chosen = jax.random.permutation(key, blocks)[partner]
    strong = (owner == chosen) | (owner == (partner + blocks // 2) % blocks)
    return jnp.where(strong, factor * values, values)


def levels(rng, dims, shards, smallest, top_value):
    loudness = 1.0
    for dim, shards_of in shards:
        draws = jax.random.uniform(jax.random.fold_in(jax.random.fold_in(rng, 6), dim), (shards_of,), jnp.float32, smallest / len(shards), top_value / len(shards))
        loudness = loudness * jnp.repeat(jnp.exp(draws), dims[dim] // shards_of).reshape((-1,) + (1,) * (len(dims) - 1 - dim))
    return loudness


def assign_block(stream_key, own, number, rows, count, top, reach, slope):
    ranking = jax.random.permutation(stream_key, count)
    crowded, ordinary = shares(count, rows * top, reach, slope, True), shares(count, rows * top, reach, slope, False)
    places = jnp.arange(count)

    def named(sizes, turn):
        used = int((sizes > 0).sum())
        fixed = max(1, used // 4)
        shifted = fixed + (places - fixed + turn * (used - fixed)) % max(1, count - fixed)
        return jnp.zeros((count,), jnp.int32).at[ranking[jnp.where(places < fixed, places, shifted)]].set(jnp.asarray(sizes, jnp.int32))

    sizes = jnp.where(number % 4 == 0, named(crowded, number // 4), named(ordinary, number - number // 4 - 1))
    mixed = jax.random.permutation(jax.random.fold_in(own, 3), count)
    giver, taker = mixed[0:count // 2 * 2:2], mixed[1:count // 2 * 2:2]
    room = jnp.minimum(sizes[giver] - 1, reach - sizes[taker]) // 2
    room = jnp.where((giver == ranking[0]) | (taker == ranking[0]) | (sizes[taker] == 0), 0, jnp.maximum(room, 0))
    shifted = jax.random.randint(jax.random.fold_in(own, 4), (count // 2,), 0, 1 << 20) % (room + 1)
    sizes = sizes.at[giver].add(-shifted).at[taker].add(shifted)
    labels = jnp.searchsorted(jnp.cumsum(sizes), jnp.arange(rows * top), side="right").astype(jnp.int32)
    table = labels.reshape(top, rows).T
    table = table[jax.random.permutation(jax.random.fold_in(own, 1), rows)]
    turn = jax.random.randint(jax.random.fold_in(own, 2), (rows, 1), 0, top)
    return jnp.take_along_axis(table, (jnp.arange(top)[None, :] + turn) % top, axis=1)


def shares(amount, total, limit, lean, full):
    portions = [(1 << 20) // math.isqrt(standing ** lean) + 1 for standing in range(1, amount + 1)]
    largest = limit if full else min(limit, max(-(-total // amount), total * portions[0] // sum(portions)))
    least = 1 if total - largest >= amount - 1 else 0
    counts, rest = [largest] + [least] * (amount - 1), total - largest - least * (amount - 1)
    while rest > 0:
        candidates = [i for i in range(1, amount) if counts[i] < largest] or [i for i in range(1, amount) if counts[i] < limit]
        pool, left = sum([portions[i] for i in candidates]), rest
        for i in candidates:
            extra = min(limit - counts[i], max(1, left * portions[i] // pool), rest)
            counts[i] = counts[i] + extra
            rest = rest - extra
    return np.array(counts)


def centred(rng, dims, deviation, bound, shards=(), kind=jnp.bfloat16):
    values = deviation * jax.random.normal(rng, dims, jnp.float32)
    if shards:
        values = values * levels(rng, dims, shards, -0.22, 0.18)
    return jnp.clip(values, -bound, bound).astype(kind)


def bell_draw_with(rng, extent, spread, most, pieces, heavy, kind=jnp.bfloat16):
    result = spread * jax.random.normal(rng, extent, jnp.float32)
    if pieces:
        result = result * levels(rng, extent, pieces, -0.22, 0.18)
    return jnp.clip(with_spikes(result, jax.random.fold_in(rng, 3), *heavy), -most, most).astype(kind)


def setup_inputs(seed: int = 0) -> dict:
    streams_of = jax.random.split(jax.random.key(seed), 9)
    query_in = centred(streams_of[0], (TOKENS, HEADS * DH), (DH ** -0.5), 0.52734375, ((0, 64), (1, 4)))
    key_in = centred(streams_of[1], (TOKENS, HEADS * DH), (DH ** -0.5), 0.52734375, ((0, 64), (1, 4)))
    value_in = centred(streams_of[2], (TOKENS, HEADS * DH), (DH ** -0.5), 0.52734375, ((0, 64), (1, 4)))
    out_grad = centred(streams_of[3], (TOKENS, HEADS * DH), ((DH / TOKENS) ** 0.5), 0.375, ((0, 64), (1, 4)))
    inputs = bell_draw_with(streams_of[4], (TOKENS, DIN), ((2 / TOKENS) ** 0.5), 0.125, ((0, 64),), (0, 1, 64, 4.0))
    expert_ids_keys = jax.random.split(jax.random.fold_in(streams_of[5], 1), TOKENS // TOK_DEV)
    expert_ids_turns = jax.random.permutation(jax.random.fold_in(streams_of[5], 3), TOKENS // TOK_DEV)
    expert_ids = jax.vmap(lambda own, number: assign_block(jax.random.fold_in(streams_of[5], 2), own, number, TOK_DEV, EXPERTS, 2, CAP, 2))(expert_ids_keys, expert_ids_turns).reshape((TOKENS, 2))
    route_gates = jnp.clip(0.2 + 0.8 * jax.random.uniform(streams_of[6], (TOKENS, 2), jnp.float32) ** levels(streams_of[6], (TOKENS, 2), ((0, 64),), -0.2, 0.2), 0.2, 1.0)
    expert_weight = centred(streams_of[7], (EXPERTS, DIN, 2 * HEADS * DH), (2 * HEADS * DH) ** -0.5, 0.09375, ((0, 4),))
    return {"query_in": query_in, "key_in": key_in, "value_in": value_in, "out_grad": out_grad, "inputs": inputs, "expert_ids": expert_ids, "route_gates": route_gates, "expert_weight": expert_weight}


highest_accuracy = lax.Precision.HIGHEST


def block_grads(backward_query, backward_key, backward_value, backward_gradient, leading_sum, trailing_sum):
    length = backward_query.shape[0]
    places = jnp.arange(length, dtype=jnp.int32)
    lower_triangle = (places[:, None] >= places[None, :])[None]
    upper_triangle = (places[:, None] <= places[None, :])[None]
    forward_query = backward_query.astype(jnp.float32)
    forward_key = backward_key.astype(jnp.float32)
    forward_value = backward_value.astype(jnp.float32)
    forward_gradient = backward_gradient.astype(jnp.float32)
    first_scores = jnp.where(lower_triangle, jnp.einsum('qnc,onc->nqo', forward_gradient, forward_value), 0.0).astype(jnp.bfloat16)
    middle_scores = jnp.where(upper_triangle, jnp.einsum('qnc,onc->nqo', forward_key, forward_query), 0.0).astype(jnp.bfloat16)
    third_scores = jnp.where(upper_triangle, jnp.einsum('qnc,onc->nqo', forward_value, forward_gradient), 0.0).astype(jnp.bfloat16)
    gradient_of_queries = jnp.einsum('wgq,qwn->gwn', first_scores.astype(jnp.float32), forward_key) + jnp.einsum('iok,osk->ios', forward_gradient, leading_sum, precision=highest_accuracy)
    gradient_of_keys = jnp.einsum('wgq,qwn->gwn', third_scores.astype(jnp.float32), forward_query) + jnp.einsum('iok,osk->ios', forward_value, trailing_sum, precision=highest_accuracy)
    value_grad = jnp.einsum('hlm,mhe->lhe', middle_scores.astype(jnp.float32), forward_gradient) + jnp.einsum('lhd,hde->lhe', forward_key, trailing_sum, precision=highest_accuracy)
    return gradient_of_queries.astype(jnp.bfloat16), gradient_of_keys.astype(jnp.bfloat16), value_grad.astype(jnp.bfloat16)


def reference(query_in, key_in, value_in, out_grad, inputs, expert_ids, route_gates, expert_weight):
    shape_four = (N_SEQ, TOK_DEV, HEADS, DH)
    backward_query = query_in.reshape(shape_four)
    backward_key = key_in.reshape(shape_four)
    backward_value = value_in.reshape(shape_four)
    backward_gradient = out_grad.reshape(shape_four)
    kv_sum = jnp.einsum('clhd,clhe->chde', backward_key.astype(jnp.float32), backward_value.astype(jnp.float32))
    qo_sum = jnp.einsum('clhd,clhe->chde', backward_query.astype(jnp.float32), backward_gradient.astype(jnp.float32))
    prefix_state = jnp.cumsum(kv_sum, axis=0) - kv_sum
    suffix_state = jnp.sum(qo_sum, axis=0)[None] - jnp.cumsum(qo_sum, axis=0)

    def one_block(packed):
        return block_grads(*packed)

    gradient_of_queries, gradient_of_keys, value_grad = lax.map(one_block, (backward_query, backward_key, backward_value, backward_gradient, prefix_state, suffix_state))
    gradient_of_queries = gradient_of_queries.reshape(TOKENS, HEADS * DH)
    gradient_of_keys = gradient_of_keys.reshape(TOKENS, HEADS * DH)
    value_grad = value_grad.reshape(TOKENS, HEADS * DH)
    kv_grad = jnp.concatenate([gradient_of_keys, value_grad], axis=1)
    input_acc = jnp.zeros((TOKENS, DIN), jnp.float32)
    weight_list = []
    for expert in range(EXPERTS):
        route_wt = jnp.sum(jnp.where(expert_ids == expert, route_gates, 0.0), axis=1)
        weighted = (route_wt[:, None] * inputs.astype(jnp.float32)).astype(jnp.bfloat16)
        weight_list.append(jnp.dot(weighted.T, kv_grad, preferred_element_type=jnp.float32))
        back_proj = lax.dot_general(kv_grad, expert_weight[expert], (((1,), (1,)), ((), ())), preferred_element_type=jnp.float32)
        input_acc = input_acc + route_wt[:, None] * back_proj
    return gradient_of_queries, gradient_of_keys, value_grad, input_acc.astype(jnp.bfloat16), jnp.stack(weight_list, axis=0)
```

```python
import jax
import jax.numpy as jnp
from jax import lax
from jax.experimental import pallas as pl
from jax.experimental.pallas import tpu as pltpu
from jax.sharding import PartitionSpec as P

MESH = pl.DeviceIdType.MESH
F32 = jnp.float32
BF16 = jnp.bfloat16
NX = 4
NY = 4
NZ = 8
NM = 2 * NY
DH = 128
HEADS = 4
TOK = 512
COL = 512
DIN = 1024
RB = 32


def mm(a, b, ca, cb):
    return lax.dot_general(a, b, (((ca,), (cb,)), ((), ())), preferred_element_type=F32)


def rcopy(src, dst, ssem, rsem, seq, exp):
    return pltpu.make_async_remote_copy(
        src_ref=src,
        dst_ref=dst,
        send_sem=ssem,
        recv_sem=rsem,
        device_id={"seq": seq, "exp": exp},
        device_id_type=MESH,
    )


def ring(count, place, neighbour, block, slots, ssem, rsem, exp, sends):
    flows = []
    for e in range(2):
        for way in range(2):
            sign = 1 if way == 0 else -1
            hops = count // 2 if (e == way) else (count - 1) // 2
            flows.append((e, way, sign, hops))
    flows.sort(key=lambda f: -f[3])
    longest = count // 2

    def go(src, e, way, sign, hop):
        copy = rcopy(
            src,
            slots.at[e, way, hop],
            ssem.at[e, way, hop],
            rsem.at[e, way, hop],
            neighbour(sign),
            exp,
        )
        copy.start()
        sends.append(copy)

    def arrived(e, way, sign, hop):
        ref = slots.at[e, way, hop]
        rcopy(ref, ref, ssem.at[e, way, hop], rsem.at[e, way, hop], neighbour(sign), exp).wait_recv()

    for hop in range(longest):
        for e, way, sign, hops in flows:
            if hop >= hops:
                continue
            dest = lax.rem(place + sign * (hops - hop) + 2 * count, count)
            if hop == 0:
                go(block(e, dest), e, way, sign, 0)
                yield ("first", hops)
            else:
                arrived(e, way, sign, hop - 1)
                ref = slots.at[e, way, hop - 1]
                ref[...] = (ref[...].astype(F32) + block(e, dest)[...].astype(F32)).astype(BF16)
                go(ref, e, way, sign, hop)
        yield ("hop", hop)
    for e in range(2):
        total = block(e, place)[...].astype(F32)
        for way in range(2):
            hops = [f[3] for f in flows if f[0] == e and f[1] == way][0]
            if hops:
                arrived(e, way, 1 if way == 0 else -1, hops - 1)
                total = total + slots[e, way, hops - 1].astype(F32)
        yield ("done", e, total)


def kernel(
    q_ref, k_ref, v_ref, do_ref, inp_ref, ids_ref, gates_ref, w_ref,
    gq_out, gk_out, gv_out, ig_out, wg_out,
    own_states, got_states, z_totals, z_own, back_states, states, base,
    intra, grads, other, gq_buf, in_own, in_other, rw_full, rw_own, rw_other,
    wy, wz, py, pz, y1, z2, z1, y2, ry, rz, fin, wg_buf,
    wx, relay, ig_acc, ig_send, ig_got, ig_buf,
    a_s, a_r, b_s, b_r, c_s, c_r, y1_s, y1_r, z2_s, z2_r, z1_s, z1_r, y2_s, y2_r,
    f_s, f_r, w_s, w_r, h_s, h_r, i_s, i_r, p_s, p_r, loc,
):
    s = lax.axis_index("seq")
    x = lax.axis_index("exp")
    m = lax.rem(s, NM)
    z = s // NM
    c = lax.rem(s, 2)
    y = m // 2
    mate = s + 1 - 2 * c
    sends = []

    def at_y(sign):
        return z * NM + lax.rem(y + sign + NY, NY) * 2 + c

    def at_z(sign):
        return lax.rem(z + sign + NZ, NZ) * NM + m

    barrier = pltpu.get_barrier_semaphore()
    peers = 0
    for d in range(1, NM):
        pl.semaphore_signal(barrier, inc=1, device_id={"seq": z * NM + lax.rem(m + d, NM), "exp": x}, device_id_type=MESH)
        peers += 1
    for d in range(1, NZ):
        pl.semaphore_signal(barrier, inc=1, device_id={"seq": lax.rem(z + d, NZ) * NM + m, "exp": x}, device_id_type=MESH)
        peers += 1
    for d in range(1, NX):
        for other_core in range(2):
            pl.semaphore_signal(barrier, inc=1, device_id={"seq": s - c + other_core, "exp": lax.rem(x + d, NX)}, device_id_type=MESH)
            peers += 1

    def w_cols(rows, part, xx):
        return w_ref.at[0, rows, pl.ds(pl.multiple_of(part * (NX * COL) + xx * COL, COL), COL)]

    own_w = [
        pltpu.make_async_copy(
            w_cols(pl.ds(0, DIN), part, x), wx.at[x, :, pl.ds(part * COL, COL)], loc.at[part]
        )
        for part in range(2)
    ]
    for copy in own_w:
        copy.start()

    def own_state(h, _):
        cols = pl.ds(pl.multiple_of(h * DH, DH), DH)
        own_states[h] = mm(k_ref[:, cols], v_ref[:, cols], 0, 0).astype(BF16)
        own_states[HEADS + h] = mm(q_ref[:, cols], do_ref[:, cols], 0, 0).astype(BF16)
        return 0

    lax.fori_loop(0, HEADS, own_state, 0)

    pl.semaphore_wait(barrier, peers)

    for d in range(1, NM):
        p = lax.rem(m + d, NM)
        copy = rcopy(own_states.at[p], got_states.at[m], a_s.at[d], a_r.at[d], z * NM + p, x)
        copy.start()
        sends.append(copy)
    got_states[m] = own_states[m]

    half = pl.ds(pl.multiple_of(c * (DIN // 2), DIN // 2), DIN // 2)
    toward = lax.rem(x + 1 + 2 * c, NX)
    across = lax.rem(x + 2, NX)
    origin = lax.rem(x + 3 - 2 * c, NX)
    for part in range(2):
        copy = rcopy(w_cols(half, part, across), relay.at[part], w_s.at[0, part], w_r.at[0, part], s, toward)
        copy.start()
        sends.append(copy)
    for way, d in ((1, 1), (2, NX - 1)):
        to = lax.rem(x + d, NX)
        for part in range(2):
            copy = rcopy(
                w_cols(half, part, to), wx.at[x, half, pl.ds(part * COL, COL)],
                w_s.at[way, part], w_r.at[way, part], s, to,
            )
            copy.start()
            sends.append(copy)

    lane = lax.broadcasted_iota(jnp.int32, (TOK, DH), 1)
    rw = jnp.where(ids_ref[:, 0:1] == lane, gates_ref[:, 0:1], 0.0) + jnp.where(
        ids_ref[:, 1:2] == lane, gates_ref[:, 1:2], 0.0
    )
    rw_full[...] = rw
    rw_own[...] = rw.T[0:8, :]

    def turn(j, _):
        cols = pl.ds(pl.multiple_of(j * DH, DH), DH)
        in_own[cols, :] = inp_ref[:, cols].astype(F32).T.astype(BF16)
        return 0

    lax.fori_loop(0, DIN // DH, turn, 0)
    for i, (src, dst) in enumerate(((in_own, in_other), (rw_own, rw_other))):
        copy = rcopy(src, dst, p_s.at[i], p_r.at[i], mate, x)
        copy.start()
        sends.append(copy)

    def inside(h, _):
        cols = pl.ds(pl.multiple_of(h * DH, DH), DH)
        qh, kh, vh, doh = q_ref[:, cols], k_ref[:, cols], v_ref[:, cols], do_ref[:, cols]
        row = lax.broadcasted_iota(jnp.int32, (TOK, TOK), 0)
        col = lax.broadcasted_iota(jnp.int32, (TOK, TOK), 1)
        first = jnp.where(row >= col, mm(doh, vh, 1, 1), 0.0).astype(BF16)
        intra[0, :, cols] = mm(first, kh, 1, 0)
        third = jnp.where(row <= col, mm(vh, doh, 1, 1), 0.0).astype(BF16)
        intra[1, :, cols] = mm(third, qh, 1, 0)
        middle = jnp.where(row <= col, mm(kh, qh, 1, 1), 0.0).astype(BF16)
        intra[2, :, cols] = mm(middle, doh, 1, 0)
        return 0

    lax.fori_loop(0, HEADS // 2, inside, 0)

    forward = m < HEADS
    for d in range(1, NM):
        rcopy(own_states.at[m], got_states.at[m], a_s.at[d], a_r.at[d], mate, x).wait_recv()
    total = got_states[0].astype(F32)
    for p in range(1, NM):
        total = total + got_states[p].astype(F32)
    z_own[...] = total.astype(BF16)
    for d in range(1, NZ):
        upward = z + d < NZ

        @pl.when(forward == upward)
        def _():
            rcopy(z_own, z_totals.at[z], b_s.at[d], b_r.at[d], lax.rem(z + d, NZ) * NM + m, x).start()

    lax.fori_loop(HEADS // 2, HEADS, inside, 0)

    def weigh(src, weights, lanes):
        def one(q, _):
            yy = lax.rem(q, NY)
            zz = q // NY
            block = src[pl.ds(pl.multiple_of(q * RB, RB), RB), :].astype(F32)
            for e in range(2):
                value = (block * weights[e : e + 1, :]).astype(BF16)
                wy[yy, pl.ds(pl.multiple_of(e * NZ * RB + zz * RB, RB), RB), lanes] = value
                value = (block * weights[2 + e : 3 + e, :]).astype(BF16)
                wz[zz, pl.ds(pl.multiple_of(e * NY * RB + yy * RB, RB), RB), lanes] = value
            return 0

        lax.fori_loop(0, NY * NZ, one, 0)

    weigh(in_own, rw_own, pl.ds(0, TOK))

    base[...] = jnp.zeros_like(base)
    for d in range(1, NZ):
        source = lax.rem(z + NZ - d, NZ)

        @pl.when(forward == (z >= d))
        def _():
            ref = z_totals.at[source]
            rcopy(ref, ref, b_s.at[d], b_r.at[d], source * NM + m, x).wait_recv()
            base[...] += ref[...].astype(F32)

    start = base[...]
    before = jnp.zeros_like(start)
    total = got_states[0].astype(F32)
    for p in range(1, NM):
        total = total + got_states[p].astype(F32)
    for p in range(NM):
        piece = got_states[p].astype(F32)
        back_states[p] = (start + jnp.where(forward, before, total - before - piece)).astype(BF16)
        before = before + piece
    for d in range(1, NM):
        p = lax.rem(m + d, NM)
        copy = rcopy(back_states.at[p], states.at[m], c_s.at[d], c_r.at[d], z * NM + p, x)
        copy.start()
        sends.append(copy)
    states[m] = back_states[m]

    rcopy(in_own, in_other, p_s.at[0], p_r.at[0], mate, x).wait_recv()
    rcopy(rw_own, rw_other, p_s.at[1], p_r.at[1], mate, x).wait_recv()
    weigh(in_other, rw_other, pl.ds(TOK, TOK))

    for d in range(1, NM):
        rcopy(back_states.at[m], states.at[m], c_s.at[d], c_r.at[d], mate, x).wait_recv()

    for h in range(HEADS):
        cols = slice(h * DH, (h + 1) * DH)
        late = states[HEADS + h]
        grads[0, :, cols] = (intra[1, :, cols] + mm(v_ref[:, cols], late, 1, 1)).astype(BF16)
        grads[1, :, cols] = (intra[2, :, cols] + mm(k_ref[:, cols], late, 1, 0)).astype(BF16)
    copy = rcopy(grads.at[1 - c], other, p_s.at[2], p_r.at[2], mate, x)
    copy.start()
    sends.append(copy)
    for h in range(HEADS):
        cols = slice(h * DH, (h + 1) * DH)
        gq_buf[:, cols] = (intra[0, :, cols] + mm(do_ref[:, cols], states[h], 1, 1)).astype(BF16)
    outs = [
        pltpu.make_async_copy(gq_buf, gq_out, loc.at[2]),
        pltpu.make_async_copy(grads.at[0], gk_out, loc.at[3]),
        pltpu.make_async_copy(grads.at[1], gv_out, loc.at[4]),
    ]
    for copy in outs:
        copy.start()

    for part in range(2):
        rcopy(relay.at[part], relay.at[part], w_s.at[0, part], w_r.at[0, part], s, toward).wait_recv()
        copy = rcopy(
            relay.at[part], wx.at[origin, half, pl.ds(part * COL, COL)],
            w_s.at[3, part], w_r.at[3, part], s, toward,
        )
        copy.start()
        sends.append(copy)

    def project(e, fresh):
        scale = jnp.sum(jnp.where(lane == e, rw_full[...], 0.0), axis=1, keepdims=True)

        def one(j, _):
            rows = pl.ds(pl.multiple_of(j * (DIN // NX), DIN // NX), DIN // NX)
            value = mm(grads[0], wx[e, rows, 0:COL], 1, 1) + mm(grads[1], wx[e, rows, COL : 2 * COL], 1, 1)
            value = scale * value
            ig_acc[j] = value if fresh else ig_acc[j] + value
            return 0

        lax.fori_loop(0, NX, one, 0)

    for copy in own_w:
        copy.wait()
    project(x, True)

    rcopy(grads.at[0], other, p_s.at[2], p_r.at[2], mate, x).wait_recv()

    def dot_y(yy):
        for part in range(2):
            rows = pl.ds(part * 256, 256)
            value = mm(wy[yy, rows, 0:TOK], grads[c], 1, 0) + mm(wy[yy, rows, TOK : 2 * TOK], other[...], 1, 0)
            py[yy, rows, :] = value.astype(BF16)

    def dot_z(zz):
        value = mm(wz[zz, :, 0:TOK], grads[c], 1, 0) + mm(wz[zz, :, TOK : 2 * TOK], other[...], 1, 0)
        pz[zz] = value.astype(BF16)

    def off_y(d):
        return lax.rem(y + d + NY, NY)

    def off_z(d):
        return lax.rem(z + d + NZ, NZ)

    ring_y1 = ring(NY, y, at_y, lambda e, d: py.at[d, pl.ds(e * NZ * RB, NZ * RB)], y1, y1_s, y1_r, x, sends)
    ring_z1 = ring(NZ, z, at_z, lambda e, d: pz.at[d, pl.ds(e * NY * RB, NY * RB)], z1, z1_s, z1_r, x, sends)
    ring_z2 = ring(
        NZ, z, at_z,
        lambda e, d: ry.at[pl.ds(pl.multiple_of(e * NZ * RB + d * RB, RB), RB)],
        z2, z2_s, z2_r, x, sends,
    )
    ring_y2 = ring(
        NY, y, at_y,
        lambda e, d: rz.at[pl.ds(pl.multiple_of(e * NY * RB + d * RB, RB), RB)],
        y2, y2_s, y2_r, x, sends,
    )

    dot_y(off_y(2))
    next(ring_y1)
    next(ring_y1)
    dot_z(off_z(4))
    next(ring_z1)
    next(ring_z1)
    dot_y(off_y(1))
    dot_y(off_y(-1))
    next(ring_y1)
    next(ring_y1)
    next(ring_y1)
    dot_z(off_z(3))
    dot_z(off_z(-3))
    next(ring_z1)
    next(ring_z1)
    next(ring_z1)
    for d in (2, -2):
        dot_z(off_z(d))
    dot_y(y)
    next(ring_z1)
    next(ring_y1)
    for d in (1, -1, 0):
        dot_z(off_z(d))
    next(ring_z1)

    def hand_over(way, e):
        for part in range(2):
            ref = wx.at[e, half, pl.ds(part * COL, COL)]
            rcopy(ref, ref, w_s.at[way, part], w_r.at[way, part], s, toward).wait_recv()
            copy = rcopy(ref, ref, h_s.at[way - 1, part], h_r.at[way - 1, part], mate, x)
            copy.start()
            sends.append(copy)

    def handed(way, e):
        mate_half = pl.ds(pl.multiple_of((1 - c) * (DIN // 2), DIN // 2), DIN // 2)
        for part in range(2):
            ref = wx.at[e, mate_half, pl.ds(part * COL, COL)]
            rcopy(ref, ref, h_s.at[way - 1, part], h_r.at[way - 1, part], mate, x).wait_recv()

    for e in range(2):
        ry[pl.ds(e * NZ * RB, NZ * RB), :] = next(ring_y1)[2].astype(BF16)
    for _ in range(5):
        next(ring_z2)
    next(ring_z1)
    next(ring_z2)

    left, right = lax.rem(x + 3, NX), lax.rem(x + 1, NX)
    hand_over(1, left)
    hand_over(2, right)
    for e in range(2):
        rz[pl.ds(e * NY * RB, NY * RB), :] = next(ring_z1)[2].astype(BF16)
    for _ in range(5):
        next(ring_y2)
    next(ring_z2)
    next(ring_y2)
    handed(1, left)
    project(left, False)
    next(ring_z2)
    handed(2, right)
    project(right, False)

    def finish(e, total):
        fin[e] = total
        for core in range(2):
            src = fin.at[e, pl.ds(core * (RB // 2), RB // 2)]
            dst = wg_buf.at[:, pl.ds(pl.multiple_of(c * (NX * COL) + x * COL, COL), COL)]
            here = jnp.logical_and(x == e, c == core)

            @pl.when(jnp.logical_not(here))
            def _():
                rcopy(src, dst, f_s.at[e, core], f_r.at[x * 2 + c], s - c + core, e).start()

            @pl.when(here)
            def _():
                dst[...] = src[...]

    for e in range(2):
        finish(2 + e, next(ring_y2)[2])
    for e in range(2):
        finish(e, next(ring_z2)[2])

    hand_over(3, across)
    handed(3, across)
    project(across, False)
    for d in range(1, NX):
        to = lax.rem(x + d, NX)
        ig_send[to] = ig_acc[to].astype(BF16)
        copy = rcopy(ig_send.at[to], ig_got.at[d], i_s.at[d], i_r.at[d], s, to)
        copy.start()
        sends.append(copy)

    for xx in range(NX):
        for core in range(2):
            here = jnp.logical_and(x == xx, c == core)

            @pl.when(jnp.logical_not(here))
            def _():
                ref = wg_buf.at[:, pl.ds(core * (NX * COL) + xx * COL, COL)]
                rcopy(ref, ref, f_s.at[0, 0], f_r.at[xx * 2 + core], mate, x).wait_recv()

    wg_copy = pltpu.make_async_copy(wg_buf, wg_out, loc.at[5])
    wg_copy.start()

    value = ig_acc[x]
    for d in range(1, NX):
        ref = ig_got.at[d]
        rcopy(ref, ref, i_s.at[d], i_r.at[d], s, left).wait_recv()
        value = value + ref[...].astype(F32)
    ig_buf[...] = value.astype(BF16)
    ig_copy = pltpu.make_async_copy(ig_buf, ig_out, loc.at[6])
    ig_copy.start()

    for copy in sends:
        copy.wait_send()
    for d in range(1, NZ):

        @pl.when(forward == (z + d < NZ))
        def _():
            rcopy(z_own, z_totals.at[z], b_s.at[d], b_r.at[d], mate, x).wait_send()

    for e in range(NX):
        for core in range(2):
            here = jnp.logical_and(x == e, c == core)

            @pl.when(jnp.logical_not(here))
            def _():
                src = fin.at[e, pl.ds(core * (RB // 2), RB // 2)]
                rcopy(src, src, f_s.at[e, core], f_r.at[0], mate, x).wait_send()

    for copy in outs:
        copy.wait()
    wg_copy.wait()
    ig_copy.wait()


def per_device(query_in, key_in, value_in, out_grad, inputs, expert_ids, route_gates, expert_weight):
    vmem = pl.BlockSpec(memory_space=pltpu.VMEM)
    anywhere = pl.BlockSpec(memory_space=pl.ANY)
    dma = pltpu.SemaphoreType.DMA

    def v(shape, dtype=BF16):
        return pltpu.VMEM(shape, dtype)

    scratch = [
        v((NM, DH, DH)), v((NM, DH, DH)), v((NZ, DH, DH)), v((DH, DH)), v((NM, DH, DH)), v((NM, DH, DH)),
        v((DH, DH), F32),
        v((3, TOK, COL), F32), v((2, TOK, COL)), v((TOK, COL)), v((TOK, COL)),
        v((DIN, TOK)), v((DIN, TOK)), v((TOK, DH), F32), v((8, TOK), F32), v((8, TOK), F32),
        v((NY, 2 * NZ * RB, 2 * TOK)), v((NZ, 2 * NY * RB, 2 * TOK)),
        v((NY, 2 * NZ * RB, COL)), v((NZ, 2 * NY * RB, COL)),
        v((2, 2, NY // 2, NZ * RB, COL)), v((2, 2, NZ // 2, RB, COL)),
        v((2, 2, NZ // 2, NY * RB, COL)), v((2, 2, NY // 2, RB, COL)),
        v((2 * NZ * RB, COL)), v((2 * NY * RB, COL)),
        v((NX, RB, COL), F32), v((RB // 2, 2 * NX * COL), F32),
        v((NX, DIN, 2 * COL)), v((2, DIN // 2, COL)),
        v((NX, TOK, DIN // NX), F32), v((NX, TOK, DIN // NX)), v((NX, TOK, DIN // NX)), v((TOK, DIN // NX)),
        dma((NM,)), dma((NM,)), dma((NZ,)), dma((NZ,)), dma((NM,)), dma((NM,)),
        dma((2, 2, NY // 2)), dma((2, 2, NY // 2)), dma((2, 2, NZ // 2)), dma((2, 2, NZ // 2)),
        dma((2, 2, NZ // 2)), dma((2, 2, NZ // 2)), dma((2, 2, NY // 2)), dma((2, 2, NY // 2)),
        dma((NX, 2)), dma((NX * 2,)), dma((4, 2)), dma((4, 2)), dma((3, 2)), dma((3, 2)),
        dma((NX,)), dma((NX,)), dma((3,)), dma((3,)), dma((7,)),
    ]
    gq, gk, gv, ig, wg = pl.pallas_call(
        kernel,
        out_shape=(
            jax.ShapeDtypeStruct((TOK, COL), BF16),
            jax.ShapeDtypeStruct((TOK, COL), BF16),
            jax.ShapeDtypeStruct((TOK, COL), BF16),
            jax.ShapeDtypeStruct((TOK, DIN // NX), BF16),
            jax.ShapeDtypeStruct((RB // 2, 2 * NX * COL), F32),
        ),
        in_specs=[vmem] * 7 + [anywhere],
        out_specs=(anywhere,) * 5,
        scratch_shapes=scratch,
        compiler_params=pltpu.CompilerParams(
            collective_id=0, has_side_effects=True, vmem_limit_bytes=60 * 1024 * 1024
        ),
    )(query_in, key_in, value_in, out_grad, inputs, expert_ids, route_gates, expert_weight)
    return gq, gk, gv, ig, wg[None]


def solution(mesh):
    return jax.shard_map(
        per_device,
        mesh=mesh,
        in_specs=(
            P("seq", "exp"), P("seq", "exp"), P("seq", "exp"), P("seq", "exp"),
            P("seq", None), P("seq", None), P("seq", None), P("exp", None, None),
        ),
        out_specs=(
            P("seq", "exp"), P("seq", "exp"), P("seq", "exp"), P("seq", "exp"), P("exp", "seq", None),
        ),
        check_vma=False,
    )
```

```python
import jax
import jax.numpy as jnp
from jax import lax
from jax.experimental import pallas as pl
from jax.experimental.pallas import tpu as pltpu
from jax.sharding import PartitionSpec as P

MESH = pl.DeviceIdType.MESH
F32 = jnp.float32
BF16 = jnp.bfloat16
NX = 4
NY = 4
NZ = 8
NM = 2 * NY
DH = 128
HEADS = 4
TOK = 512
COL = 512
DIN = 1024
RB = 32


def mm(a, b, ca, cb):
    return lax.dot_general(a, b, (((ca,), (cb,)), ((), ())), preferred_element_type=F32)


def rcopy(src, dst, ssem, rsem, seq, exp):
    return pltpu.make_async_remote_copy(
        src_ref=src,
        dst_ref=dst,
        send_sem=ssem,
        recv_sem=rsem,
        device_id={"seq": seq, "exp": exp},
        device_id_type=MESH,
    )


def ring(count, place, neighbour, block, slots, ssem, rsem, drains):
    flows, base = [], {}
    for e in range(2):
        for way in range(2):
            sign = 1 if way == 0 else -1
            hops = count // 2 if (e == way) else (count - 1) // 2
            base[e, way] = sum(f[3] for f in flows)
            flows.append((e, way, sign, hops))
    far_first = sorted(flows, key=lambda f: -f[3])
    drains.append((slots, ssem))

    def go(src, e, way, sign, hop):
        seq, exp = neighbour(sign)
        i = base[e, way] + hop
        rcopy(src, slots.at[i], ssem, rsem.at[i], seq, exp).start()

    def arrived(e, way, sign, hop):
        seq, exp = neighbour(sign)
        i = base[e, way] + hop
        rcopy(slots.at[i], slots.at[i], ssem, rsem.at[i], seq, exp).wait_recv()
        return slots.at[i]

    for hop in range(count // 2):
        for e, way, sign, hops in far_first:
            if hop >= hops:
                continue
            dest = lax.rem(place + sign * (hops - hop) + 2 * count, count)
            if hop == 0:
                go(block(e, dest), e, way, sign, 0)
                yield None
            else:
                ref = arrived(e, way, sign, hop - 1)
                ref[...] = (ref[...].astype(F32) + block(e, dest)[...].astype(F32)).astype(BF16)
                go(ref, e, way, sign, hop)
        yield None
    for e in range(2):
        total = block(e, place)[...].astype(F32)
        for f in flows:
            if f[0] == e:
                total = total + arrived(*f[:3], f[3] - 1)[...].astype(F32)
        yield total


def step(generator, times=1):
    for _ in range(times):
        value = next(generator)
    return value


def kernel(
    q_in, k_in, v_in, do_in, inp_in, ids_in, gates_in, w_ref,
    gq_out, gk_out, gv_out, ig_out, wg_out,
    q_ref, k_ref, v_ref, do_ref, inp_ref, ids_ref, gates_ref,
    own_states, got_states, z_totals, z_own, back_states, states, base,
    intra, grads, other, gq_buf, in_own, in_other, rw_full, rw_own, rw_other,
    wy, wz, py, pz, y1, z2, z1, y2, xr, ry, rz, fin, wg_buf,
    wx, relay, far_grads, ig_acc, ig_send, ig_buf,
    a_s, a_r, b_s, b_r, c_s, c_r, y1_s, y1_r, z2_s, z2_r, z1_s, z1_r, y2_s, y2_r, x_s, x_r,
    f_s, f_r, w_s, w_r, h_s, h_r, k_s, k_r, p_s, p_r, loc, load,
):
    s = lax.axis_index("seq")
    x = lax.axis_index("exp")
    m = lax.rem(s, NM)
    z = s // NM
    c = lax.rem(s, 2)
    y = m // 2
    mate = s + 1 - 2 * c
    sends, drains = [], []
    most = pl.ds(0, NM - 1)

    def at_y(sign):
        return z * NM + lax.rem(y + sign + NY, NY) * 2 + c, x

    def at_z(sign):
        return lax.rem(z + sign + NZ, NZ) * NM + m, x

    def at_x(sign):
        return s, lax.rem(x + sign + NX, NX)

    barrier = pltpu.get_barrier_semaphore()
    peers = 0
    for d in range(1, NM):
        pl.semaphore_signal(barrier, inc=1, device_id={"seq": z * NM + lax.rem(m + d, NM), "exp": x}, device_id_type=MESH)
        peers += 1
    for d in range(1, NZ):
        pl.semaphore_signal(barrier, inc=1, device_id={"seq": lax.rem(z + d, NZ) * NM + m, "exp": x}, device_id_type=MESH)
        peers += 1
    for d in range(1, NX):
        for other_core in range(2):
            pl.semaphore_signal(barrier, inc=1, device_id={"seq": s - c + other_core, "exp": lax.rem(x + d, NX)}, device_id_type=MESH)
            peers += 1

    pairs = (
        (k_in, k_ref), (v_in, v_ref), (q_in, q_ref), (do_in, do_ref),
        (ids_in, ids_ref), (gates_in, gates_ref), (inp_in, inp_ref),
    )
    loads = [pltpu.make_async_copy(src, dst, load.at[i]) for i, (src, dst) in enumerate(pairs)]
    for copy in loads[:4]:
        copy.start()

    for copy in loads[:2]:
        copy.wait()

    def own_kv(h, _):
        cols = pl.ds(pl.multiple_of(h * DH, DH), DH)
        own_states[2 * h] = mm(k_ref[:, cols], v_ref[:, cols], 0, 0).astype(BF16)
        return 0

    lax.fori_loop(0, HEADS, own_kv, 0)
    for copy in loads[2:4]:
        copy.wait()
    for copy in loads[4:]:
        copy.start()

    def own_qo(h, _):
        cols = pl.ds(pl.multiple_of(h * DH, DH), DH)
        own_states[2 * h + 1] = mm(q_ref[:, cols], do_ref[:, cols], 0, 0).astype(BF16)
        return 0

    lax.fori_loop(0, HEADS, own_qo, 0)

    pl.semaphore_wait(barrier, peers)

    for d in range(1, NM):
        p = lax.rem(m + d, NM)
        rcopy(own_states.at[p], got_states.at[m], a_s, a_r, z * NM + p, x).start()
    got_states[m] = own_states[m]

    def w_cols(rows, part, xx):
        return w_ref.at[0, rows, pl.ds(pl.multiple_of(part * (NX * COL) + xx * COL, COL), COL)]

    half = pl.ds(pl.multiple_of(c * (DIN // 2), DIN // 2), DIN // 2)
    left, right = lax.rem(x + 3, NX), lax.rem(x + 1, NX)
    toward = lax.rem(x + 1 + 2 * c, NX)
    across = lax.rem(x + 2, NX)
    for part in range(2):
        for way, to in ((0, right), (1, left)):
            rcopy(w_cols(half, part, to), wx.at[x, half, pl.ds(part * COL, COL)], w_s, w_r.at[way], s, to).start()
    drains.append((wx.at[0], w_s))

    for copy in loads[4:]:
        copy.wait()
    lane = lax.broadcasted_iota(jnp.int32, (TOK, DH), 1)
    expert = lax.broadcasted_iota(jnp.int32, (DH, TOK), 0)
    rw = jnp.where(ids_ref[0:1, :] == expert, gates_ref[0:1, :], 0.0) + jnp.where(
        ids_ref[1:2, :] == expert, gates_ref[1:2, :], 0.0
    )
    rw_full[...] = rw.T
    rw_own[...] = rw[0:8, :]

    def turn(j, _):
        cols = pl.ds(pl.multiple_of(j * DH, DH), DH)
        in_own[cols, :] = inp_ref[:, cols].astype(F32).T.astype(BF16)
        return 0

    lax.fori_loop(0, DIN // DH, turn, 0)
    for i, (src, dst) in enumerate(((in_own, in_other), (rw_own, rw_other))):
        copy = rcopy(src, dst, p_s.at[i], p_r.at[i], mate, x)
        copy.start()
        sends.append(copy)

    own_w = [
        pltpu.make_async_copy(
            w_cols(pl.ds(0, DIN), part, xx), wx.at[slot, :, pl.ds(part * COL, COL)], loc.at[0]
        )
        for xx, slot in ((x, across), (across, x))
        for part in range(2)
    ]

    def inside(h, _):
        cols = pl.ds(pl.multiple_of(h * DH, DH), DH)
        qh, kh, vh, doh = q_ref[:, cols], k_ref[:, cols], v_ref[:, cols], do_ref[:, cols]
        row = lax.broadcasted_iota(jnp.int32, (TOK, TOK), 0)
        col = lax.broadcasted_iota(jnp.int32, (TOK, TOK), 1)
        first = jnp.where(row >= col, mm(doh, vh, 1, 1), 0.0).astype(BF16)
        intra[0, :, cols] = mm(first, kh, 1, 0)
        third = jnp.where(row <= col, mm(vh, doh, 1, 1), 0.0).astype(BF16)
        intra[1, :, cols] = mm(third, qh, 1, 0)
        middle = jnp.where(row <= col, mm(kh, qh, 1, 1), 0.0).astype(BF16)
        intra[2, :, cols] = mm(middle, doh, 1, 0)
        return 0

    lax.fori_loop(0, HEADS // 2, inside, 0)

    forward = c == 0
    rcopy(own_states.at[most], got_states.at[most], a_s, a_r, mate, x).wait_recv()
    drains.append((own_states.at[most], a_s))
    total = got_states[0].astype(F32)
    for p in range(1, NM):
        total = total + got_states[p].astype(F32)
    z_own[...] = total.astype(BF16)
    for d in range(1, NZ):
        upward = z + d < NZ

        @pl.when(forward == upward)
        def _():
            rcopy(z_own, z_totals.at[z], b_s.at[d], b_r.at[d], lax.rem(z + d, NZ) * NM + m, x).start()

    for copy in own_w:
        copy.start()
    lax.fori_loop(HEADS // 2, HEADS, inside, 0)

    def weigh(src, weights, lanes):
        def one(q, _):
            yy = lax.rem(q, NY)
            zz = q // NY
            block = src[pl.ds(pl.multiple_of(q * RB, RB), RB), :].astype(F32)
            for e in range(2):
                value = (block * weights[e : e + 1, :]).astype(BF16)
                wy[yy, pl.ds(pl.multiple_of(e * NZ * RB + zz * RB, RB), RB), lanes] = value
                value = (block * weights[2 + e : 3 + e, :]).astype(BF16)
                wz[zz, pl.ds(pl.multiple_of(e * NY * RB + yy * RB, RB), RB), lanes] = value
            return 0

        lax.fori_loop(0, NY * NZ, one, 0)

    weigh(in_own, rw_own, pl.ds(0, TOK))

    base[...] = jnp.zeros_like(base)
    for d in range(1, NZ):
        source = lax.rem(z + NZ - d, NZ)

        @pl.when(forward == (z >= d))
        def _():
            ref = z_totals.at[source]
            rcopy(ref, ref, b_s.at[d], b_r.at[d], source * NM + m, x).wait_recv()
            base[...] += ref[...].astype(F32)

    start = base[...]
    before = jnp.zeros_like(start)
    total = got_states[0].astype(F32)
    for p in range(1, NM):
        total = total + got_states[p].astype(F32)
    for p in range(NM):
        piece = got_states[p].astype(F32)
        back_states[p] = (start + jnp.where(forward, before, total - before - piece)).astype(BF16)
        before = before + piece
    for d in range(1, NM):
        p = lax.rem(m + d, NM)
        rcopy(back_states.at[p], states.at[m], c_s, c_r, z * NM + p, x).start()
    states[m] = back_states[m]

    rcopy(in_own, in_other, p_s.at[0], p_r.at[0], mate, x).wait_recv()
    rcopy(rw_own, rw_other, p_s.at[1], p_r.at[1], mate, x).wait_recv()
    weigh(in_other, rw_other, pl.ds(TOK, TOK))

    rcopy(back_states.at[most], states.at[most], c_s, c_r, mate, x).wait_recv()
    drains.append((back_states.at[most], c_s))

    for h in range(HEADS):
        cols = slice(h * DH, (h + 1) * DH)
        late = states[2 * h + 1]
        grads[0, :, cols] = (intra[1, :, cols] + mm(v_ref[:, cols], late, 1, 1)).astype(BF16)
        grads[1, :, cols] = (intra[2, :, cols] + mm(k_ref[:, cols], late, 1, 0)).astype(BF16)
    copy = rcopy(grads.at[1 - c], other, p_s.at[2], p_r.at[2], mate, x)
    copy.start()
    sends.append(copy)

    def tokens(part):
        return pl.ds(part * (TOK // 2), TOK // 2)

    for part in range(2):
        rcopy(grads.at[:, tokens(part)], relay.at[:, tokens(part)], k_s, k_r.at[0, part], s, toward).start()
    drains.append((wx.at[0], k_s))

    def pass_on(part):
        ref = relay.at[:, tokens(part)]
        rcopy(ref, ref, k_s, k_r.at[0, part], s, toward).wait_recv()
        rcopy(ref, far_grads.at[:, tokens(part)], k_s, k_r.at[1, part], s, toward).start()

    for h in range(HEADS):
        cols = slice(h * DH, (h + 1) * DH)
        gq_buf[:, cols] = (intra[0, :, cols] + mm(do_ref[:, cols], states[2 * h], 1, 1)).astype(BF16)
    outs = [
        pltpu.make_async_copy(gq_buf, gq_out, loc.at[1]),
        pltpu.make_async_copy(grads.at[0], gk_out, loc.at[2]),
        pltpu.make_async_copy(grads.at[1], gv_out, loc.at[3]),
    ]
    for copy in outs:
        copy.start()

    def scale_of(e, rows):
        return jnp.sum(jnp.where(lane[rows] == e, rw_full[rows, :], 0.0), axis=1, keepdims=True)

    def project(e, slot, fresh):
        scale = scale_of(e, slice(0, TOK))

        def one(j, _):
            rows = pl.ds(pl.multiple_of(j * (DIN // NX), DIN // NX), DIN // NX)
            value = mm(grads[0], wx[slot, rows, 0:COL], 1, 1) + mm(grads[1], wx[slot, rows, COL : 2 * COL], 1, 1)
            value = scale * value
            ig_acc[j] = value if fresh else ig_acc[j] + value
            return 0

        lax.fori_loop(0, NX, one, 0)

    pltpu.make_async_copy(wx.at[pl.ds(0, 2)], wx.at[pl.ds(0, 2)], loc.at[0]).wait()
    project(x, across, True)

    rcopy(grads.at[0], other, p_s.at[2], p_r.at[2], mate, x).wait_recv()

    def dot_y(d):
        yy = lax.rem(y + d + NY, NY)
        for part in range(2):
            rows = pl.ds(part * 256, 256)
            value = mm(wy[yy, rows, 0:TOK], grads[c], 1, 0) + mm(wy[yy, rows, TOK : 2 * TOK], other[...], 1, 0)
            value = value.astype(BF16)
            py[0, yy, rows, :] = value[:, : COL // 2]
            py[1, yy, rows, :] = value[:, COL // 2 :]

    def dot_z(d):
        zz = lax.rem(z + d + NZ, NZ)
        value = mm(wz[zz, :, 0:TOK], grads[c], 1, 0) + mm(wz[zz, :, TOK : 2 * TOK], other[...], 1, 0)
        value = value.astype(BF16)
        pz[0, zz] = value[:, : COL // 2]
        pz[1, zz] = value[:, COL // 2 :]

    def rows_at(ref, u, offset):
        return ref.at[u, pl.ds(pl.multiple_of(offset, RB), RB)]

    ring_y1 = [
        ring(NY, y, at_y, lambda e, d, u=u: py.at[u, d, pl.ds(e * NZ * RB, NZ * RB)], y1.at[u], y1_s.at[u], y1_r.at[u], drains)
        for u in range(2)
    ]
    ring_z1 = [
        ring(NZ, z, at_z, lambda e, d, u=u: pz.at[u, d, pl.ds(e * NY * RB, NY * RB)], z1.at[u], z1_s.at[u], z1_r.at[u], drains)
        for u in range(2)
    ]
    ring_z2 = [
        ring(NZ, z, at_z, lambda e, d, u=u: rows_at(ry, u, e * NZ * RB + d * RB), z2.at[u], z2_s.at[u], z2_r.at[u], drains)
        for u in range(2)
    ]
    ring_y2 = [
        ring(NY, y, at_y, lambda e, d, u=u: rows_at(rz, u, e * NY * RB + d * RB), y2.at[u], y2_s.at[u], y2_r.at[u], drains)
        for u in range(2)
    ]
    ring_x = [
        ring(
            NX, x, at_x,
            lambda e, d, u=u: ig_send.at[d, pl.ds(u * (TOK // 2) + e * (TOK // 4), TOK // 4)],
            xr.at[u], x_s.at[u], x_r.at[u], drains,
        )
        for u in range(2)
    ]

    def y1_done(u):
        for e in range(2):
            ry[u, pl.ds(e * NZ * RB, NZ * RB), :] = step(ring_y1[u]).astype(BF16)
        step(ring_z2[u], 5)

    def z1_done(u):
        for e in range(2):
            rz[u, pl.ds(e * NY * RB, NY * RB), :] = step(ring_z1[u]).astype(BF16)
        step(ring_y2[u], 5)

    def hand_over(way, e):
        ref = wx.at[e, half]
        rcopy(ref, ref, w_s, w_r.at[way], s, toward).wait_recv()
        rcopy(ref, ref, h_s, h_r.at[way], mate, x).start()

    drains.append((wx.at[0], h_s))

    def handed(way, e):
        ref = wx.at[e, pl.ds(pl.multiple_of((1 - c) * (DIN // 2), DIN // 2), DIN // 2)]
        rcopy(ref, ref, h_s, h_r.at[way], mate, x).wait_recv()

    def last_project(u):
        ref = far_grads.at[:, tokens(u)]
        rcopy(ref, ref, k_s, k_r.at[1, u], s, toward).wait_recv()
        scale = scale_of(x, slice(u * (TOK // 2), (u + 1) * (TOK // 2)))

        def one(j, _):
            rows = pl.ds(pl.multiple_of(j * (DIN // NX), DIN // NX), DIN // NX)
            value = mm(far_grads[0, tokens(u), :], wx[x, rows, 0:COL], 1, 1) + mm(
                far_grads[1, tokens(u), :], wx[x, rows, COL : 2 * COL], 1, 1
            )
            ig_send[j, tokens(u), :] = (ig_acc[j, tokens(u), :] + scale * value).astype(BF16)
            return 0

        lax.fori_loop(0, NX, one, 0)
        step(ring_x[u], 5)

    def finish(e, u, total):
        fin[u, e] = total
        for core in range(2):
            src = fin.at[u, e, pl.ds(core * (RB // 2), RB // 2)]
            first = c * (NX * COL) + x * COL + u * (COL // 2)
            dst = wg_buf.at[:, pl.ds(pl.multiple_of(first, COL // 2), COL // 2)]
            here = jnp.logical_and(x == e, c == core)

            @pl.when(jnp.logical_not(here))
            def _():
                rcopy(src, dst, f_s, f_r, s - c + core, e).start()

            @pl.when(here)
            def _():
                dst[...] = src[...]

    def finish_y(u):
        for e in range(2):
            finish(2 + e, u, step(ring_y2[u]))

    def finish_z(u):
        for e in range(2):
            finish(e, u, step(ring_z2[u]))

    def ig_done(u):
        for e in range(2):
            ig_buf[pl.ds(u * (TOK // 2) + e * (TOK // 4), TOK // 4), :] = step(ring_x[u]).astype(BF16)

    dot_y(2)
    step(ring_y1[0], 2)
    dot_z(4)
    step(ring_z1[0], 2)
    step(ring_z1[1], 2)
    dot_y(1)
    dot_y(-1)
    step(ring_y1[0], 3)
    dot_z(3)
    dot_z(-3)
    step(ring_z1[0], 3)
    step(ring_z1[1], 3)
    dot_z(2)
    dot_z(-2)
    dot_y(0)
    hand_over(0, left)
    hand_over(1, right)
    step(ring_y1[0])
    step(ring_y1[1], 5)
    step(ring_z1[0])
    dot_z(1)
    dot_z(-1)
    step(ring_z1[1])
    dot_z(0)
    handed(0, left)
    project(left, left, False)
    step(ring_z1[0])
    y1_done(0)
    pass_on(0)
    step(ring_z1[1])
    step(ring_y1[1])
    pass_on(1)
    step(ring_z2[0])
    handed(1, right)
    project(right, right, False)
    step(ring_z1[0])
    step(ring_z1[1])
    step(ring_z2[0])
    y1_done(1)
    z1_done(0)
    step(ring_z2[0])
    z1_done(1)
    step(ring_z2[1])
    step(ring_y2[0])
    last_project(0)
    step(ring_z2[1])
    step(ring_y2[1])
    finish_z(0)
    finish_y(0)
    step(ring_z2[1])
    step(ring_x[0])
    finish_y(1)
    last_project(1)
    finish_z(1)
    ig_done(0)
    step(ring_x[1])
    arriving = wg_buf.at[:, pl.ds(0, 2 * (2 * NX - 1) * (COL // 2))]
    rcopy(arriving, arriving, f_s, f_r, mate, x).wait_recv()
    drains.append((arriving, f_s))
    outs.append(pltpu.make_async_copy(wg_buf, wg_out, loc.at[4]))
    outs[-1].start()
    ig_done(1)
    outs.append(pltpu.make_async_copy(ig_buf, ig_out, loc.at[5]))
    outs[-1].start()

    for copy in sends:
        copy.wait_send()
    for d in range(1, NZ):

        @pl.when(forward == (z + d < NZ))
        def _():
            rcopy(z_own, z_totals.at[z], b_s.at[d], b_r.at[d], mate, x).wait_send()

    for ref, sem in drains:
        rcopy(ref, ref, sem, a_r, mate, x).wait_send()
    for copy in outs:
        copy.wait()


def write_out(*refs):
    sems = refs[10]
    copies = [pltpu.make_async_copy(refs[i], refs[5 + i], sems.at[i]) for i in range(5)]
    for copy in copies:
        copy.start()
    for copy in copies:
        copy.wait()


def per_device(query_in, key_in, value_in, out_grad, inputs, expert_ids, route_gates, expert_weight):
    vmem = pl.BlockSpec(memory_space=pltpu.VMEM)
    anywhere = pl.BlockSpec(memory_space=pl.ANY)
    dma = pltpu.SemaphoreType.DMA

    def v(shape, dtype=BF16):
        return pltpu.VMEM(shape, dtype)

    scratch = [
        v((TOK, COL)), v((TOK, COL)), v((TOK, COL)), v((TOK, COL)), v((TOK, DIN)), v((2, TOK), jnp.int32), v((2, TOK), F32),
        v((NM, DH, DH)), v((NM, DH, DH)), v((NZ, DH, DH)), v((DH, DH)), v((NM, DH, DH)), v((NM, DH, DH)),
        v((DH, DH), F32),
        v((3, TOK, COL), F32), v((2, TOK, COL)), v((TOK, COL)), v((TOK, COL)),
        v((DIN, TOK)), v((DIN, TOK)), v((TOK, DH), F32), v((8, TOK), F32), v((8, TOK), F32),
        v((NY, 2 * NZ * RB, 2 * TOK)), v((NZ, 2 * NY * RB, 2 * TOK)),
        v((2, NY, 2 * NZ * RB, COL // 2)), v((2, NZ, 2 * NY * RB, COL // 2)),
        v((2, 2 * (NY - 1), NZ * RB, COL // 2)), v((2, 2 * (NZ - 1), RB, COL // 2)),
        v((2, 2 * (NZ - 1), NY * RB, COL // 2)), v((2, 2 * (NY - 1), RB, COL // 2)),
        v((2, 2 * (NX - 1), TOK // 4, DIN // NX)),
        v((2, 2 * NZ * RB, COL // 2)), v((2, 2 * NY * RB, COL // 2)),
        v((2, NX, RB, COL // 2), F32), v((RB // 2, 2 * NX * COL), F32),
        v((NX, DIN, 2 * COL)), v((2, TOK, COL)), v((2, TOK, COL)),
        v((NX, TOK, DIN // NX), F32), v((NX, TOK, DIN // NX)), v((TOK, DIN // NX)),
        dma(()), dma(()), dma((NZ,)), dma((NZ,)), dma(()), dma(()),
        dma((2,)), dma((2, 2 * (NY - 1))), dma((2,)), dma((2, 2 * (NZ - 1))),
        dma((2,)), dma((2, 2 * (NZ - 1))), dma((2,)), dma((2, 2 * (NY - 1))),
        dma((2,)), dma((2, 2 * (NX - 1))),
        dma(()), dma(()), dma(()), dma((2,)), dma(()), dma((2,)),
        dma(()), dma((2, 2)), dma((3,)), dma((3,)), dma((6,)), dma((7,)),
    ]
    gq, gk, gv, ig, wg = pl.pallas_call(
        kernel,
        out_shape=(
            pltpu.VMEM((TOK, COL), BF16),
            pltpu.VMEM((TOK, COL), BF16),
            pltpu.VMEM((TOK, COL), BF16),
            pltpu.VMEM((TOK, DIN // NX), BF16),
            pltpu.VMEM((RB // 2, 2 * NX * COL), F32),
        ),
        in_specs=[anywhere] * 8,
        out_specs=(anywhere,) * 5,
        scratch_shapes=scratch,
        compiler_params=pltpu.CompilerParams(
            collective_id=0, has_side_effects=True, vmem_limit_bytes=56 * 1024 * 1024
        ),
    )(query_in, key_in, value_in, out_grad, inputs, expert_ids.T, route_gates.T, expert_weight)
    gq, gk, gv, ig, wg = pl.pallas_call(
        write_out,
        out_shape=tuple(jax.ShapeDtypeStruct(a.shape, a.dtype) for a in (gq, gk, gv, ig, wg)),
        in_specs=[vmem] * 5,
        out_specs=(anywhere,) * 5,
        scratch_shapes=[dma((5,))],
    )(*(pltpu.with_memory_space_constraint(a, pltpu.VMEM) for a in (gq, gk, gv, ig, wg)))
    return gq, gk, gv, ig, wg[None]


def solution(mesh):
    return jax.shard_map(
        per_device,
        mesh=mesh,
        in_specs=(
            P("seq", "exp"), P("seq", "exp"), P("seq", "exp"), P("seq", "exp"),
            P("seq", None), P("seq", None), P("seq", None), P("exp", None, None),
        ),
        out_specs=(
            P("seq", "exp"), P("seq", "exp"), P("seq", "exp"), P("seq", "exp"), P("exp", "seq", None),
        ),
        check_vma=False,
    )
```

```python
import jax
import jax.numpy as jnp
from jax import lax
from jax.experimental import pallas as pl
from jax.experimental.pallas import tpu as pltpu
from jax.sharding import PartitionSpec as P

MESH = pl.DeviceIdType.MESH
F32 = jnp.float32
BF16 = jnp.bfloat16
NX = 4
NY = 4
NZ = 8
NM = 2 * NY
DH = 128
HEADS = 4
TOK = 512
COL = 512
DIN = 1024
RB = 32


def mm(a, b, ca, cb):
    return lax.dot_general(a, b, (((ca,), (cb,)), ((), ())), preferred_element_type=F32)


def rcopy(src, dst, ssem, rsem, seq, exp):
    return pltpu.make_async_remote_copy(
        src_ref=src,
        dst_ref=dst,
        send_sem=ssem,
        recv_sem=rsem,
        device_id={"seq": seq, "exp": exp},
        device_id_type=MESH,
    )


def ring(count, place, neighbour, block, slots, ssem, rsem, drains):
    pairs = []
    for far in (True, False):
        hops = count // 2 if far else (count - 1) // 2
        pairs.append((hops, [(e, 1 if (e == 0) == far else -1) for e in range(2)]))
    drains.append((slots, ssem))

    def index(pair, hop):
        return hop + (0 if pair == 0 else pairs[0][0])

    def go(src, pair, i, hop):
        seq, exp = neighbour(pairs[pair][1][i][1])
        at = index(pair, hop)
        rcopy(src, slots.at[at, i], ssem, rsem.at[at], seq, exp).start()

    def arrived(pair, hop):
        seq, exp = neighbour(1)
        at = index(pair, hop)
        rcopy(slots.at[at], slots.at[at], ssem, rsem.at[at], seq, exp).wait_recv()

    for hop in range(count // 2):
        for pair, (hops, flows) in enumerate(pairs):
            if hop >= hops:
                continue
            if hop:
                arrived(pair, hop - 1)
            for i, (e, sign) in enumerate(flows):
                dest = lax.rem(place + sign * (hops - hop) + 2 * count, count)
                if hop:
                    ref = slots.at[index(pair, hop - 1), i]
                    ref[...] = (ref[...].astype(F32) + block(e, dest)[...].astype(F32)).astype(BF16)
                    go(ref, pair, i, hop)
                else:
                    go(block(e, dest), pair, i, 0)
            if not hop:
                yield None
        if hop:
            yield None
    for pair, (hops, _) in enumerate(pairs):
        arrived(pair, hops - 1)
    for e in range(2):
        total = block(e, place)[...].astype(F32)
        for pair, (hops, _) in enumerate(pairs):
            total = total + slots[index(pair, hops - 1), e].astype(F32)
        yield total


def step(generator, times=1):
    for _ in range(times):
        value = next(generator)
    return value


def kernel(
    q_in, k_in, v_in, do_in, inp_in, ids_in, gates_in, w_ref,
    gq_out, gk_out, gv_out, ig_out, wg_out,
    q_ref, k_ref, v_ref, do_ref, inp_ref, ids_ref, gates_ref,
    own_states, got_states, z_totals, z_own, back_states, states, base,
    intra, grads, other, gq_buf, in_own, in_other, rw_full, rw_own, rw_other,
    wy, wz, py, pz, y1, z2, z1, y2, xr, ry, rz, fin, wg_buf,
    wx, relay, far_grads, ig_acc, ig_send, ig_buf,
    a_s, a_r, b_s, b_r, c_s, c_r, y1_s, y1_r, z2_s, z2_r, z1_s, z1_r, y2_s, y2_r, x_s, x_r,
    f_s, f_r, w_s, w_s2, w_r, h_s, h_r, k_s, k_r, p_s, p_r, loc, load,
):
    s = lax.axis_index("seq")
    x = lax.axis_index("exp")
    m = lax.rem(s, NM)
    z = s // NM
    c = lax.rem(s, 2)
    y = m // 2
    mate = s + 1 - 2 * c
    sends, drains = [], []
    most = pl.ds(0, NM - 1)

    def at_y(sign):
        return z * NM + lax.rem(y + sign + NY, NY) * 2 + c, x

    def at_z(sign):
        return lax.rem(z + sign + NZ, NZ) * NM + m, x

    def at_x(sign):
        return s, lax.rem(x + sign + NX, NX)

    barrier = pltpu.get_barrier_semaphore()
    peers = 0
    for d in range(1, NM):
        pl.semaphore_signal(barrier, inc=1, device_id={"seq": z * NM + lax.rem(m + d, NM), "exp": x}, device_id_type=MESH)
        peers += 1
    for d in range(1, NZ):
        pl.semaphore_signal(barrier, inc=1, device_id={"seq": lax.rem(z + d, NZ) * NM + m, "exp": x}, device_id_type=MESH)
        peers += 1
    for d in range(1, NX):
        for other_core in range(2):
            pl.semaphore_signal(barrier, inc=1, device_id={"seq": s - c + other_core, "exp": lax.rem(x + d, NX)}, device_id_type=MESH)
            peers += 1

    pairs = (
        (k_in, k_ref), (v_in, v_ref), (q_in, q_ref), (do_in, do_ref),
        (ids_in, ids_ref), (gates_in, gates_ref), (inp_in, inp_ref),
    )
    loads = [pltpu.make_async_copy(src, dst, load.at[i]) for i, (src, dst) in enumerate(pairs)]
    for copy in loads[:4]:
        copy.start()

    for copy in loads[:2]:
        copy.wait()

    def own_kv(h, _):
        cols = pl.ds(pl.multiple_of(h * DH, DH), DH)
        own_states[2 * h] = mm(k_ref[:, cols], v_ref[:, cols], 0, 0).astype(BF16)
        return 0

    lax.fori_loop(0, HEADS, own_kv, 0)
    for copy in loads[2:4]:
        copy.wait()
    for copy in loads[4:]:
        copy.start()

    def own_qo(h, _):
        cols = pl.ds(pl.multiple_of(h * DH, DH), DH)
        own_states[2 * h + 1] = mm(q_ref[:, cols], do_ref[:, cols], 0, 0).astype(BF16)
        return 0

    lax.fori_loop(0, HEADS, own_qo, 0)

    pl.semaphore_wait(barrier, peers)

    def part_of(u):
        return pl.ds(u * (DH // 2), DH // 2)

    for u in range(2):
        for d in range(1, NM):
            p = lax.rem(m + d, NM)
            rcopy(own_states.at[p, part_of(u)], got_states.at[m, part_of(u)], a_s, a_r.at[u], z * NM + p, x).start()
    got_states[m] = own_states[m]

    def w_cols(rows, part, xx):
        return w_ref.at[0, rows, pl.ds(pl.multiple_of(part * (NX * COL) + xx * COL, COL), COL)]

    start_row = c * (DIN // 2)
    half = pl.ds(pl.multiple_of(start_row, DIN // 2), DIN // 2)
    left, right = lax.rem(x + 3, NX), lax.rem(x + 1, NX)
    toward = lax.rem(x + 1 + 2 * c, NX)
    across = lax.rem(x + 2, NX)
    odd = lax.rem(z, 2)

    def w_rows(offset, count):
        return pl.ds(pl.multiple_of(start_row + offset, 64), count)

    shared = w_rows(256 + 128 * odd, 128)
    for rows, sem in ((shared, 0), (w_rows(0, 256), 1)):
        for to in (right, left):
            for part in range(2):
                rcopy(w_cols(rows, part, to), wx.at[x, rows, pl.ds(part * COL, COL)], w_s, w_r.at[sem], s, to).start()
    drains.append((wx.at[0, pl.ds(0, 768)], w_s))

    def share_weights():
        ref = wx.at[0, pl.ds(0, 256)]
        rcopy(ref, ref, w_s, w_r.at[0], s, toward).wait_recv()
        for e in (left, right):
            for i, sign in ((0, 1 - 2 * odd), (1, 2 * odd - 1)):
                ref = wx.at[e, w_rows(256 + 128 * odd + 64 * i, 64)]
                seq, exp = at_z(sign)
                rcopy(ref, ref, w_s2, w_r.at[2], seq, exp).start()
        drains.append((wx.at[0, pl.ds(0, 256)], w_s2))

    def all_weights():
        ref = wx.at[0, pl.ds(0, 512)]
        rcopy(ref, ref, w_s, w_r.at[1], s, toward).wait_recv()
        ref = wx.at[0, pl.ds(0, 256)]
        rcopy(ref, ref, w_s, w_r.at[2], s, toward).wait_recv()

    for copy in loads[4:]:
        copy.wait()
    lane = lax.broadcasted_iota(jnp.int32, (TOK, DH), 1)
    expert = lax.broadcasted_iota(jnp.int32, (DH, TOK), 0)
    rw = jnp.where(ids_ref[0:1, :] == expert, gates_ref[0:1, :], 0.0) + jnp.where(
        ids_ref[1:2, :] == expert, gates_ref[1:2, :], 0.0
    )
    rw_full[...] = rw.T
    rw_own[...] = rw[0:8, :]

    def turn(j, _):
        cols = pl.ds(pl.multiple_of(j * DH, DH), DH)
        in_own[cols, :] = inp_ref[:, cols].astype(F32).T.astype(BF16)
        return 0

    lax.fori_loop(0, DIN // DH, turn, 0)
    for i, (src, dst) in enumerate(((in_own, in_other), (rw_own, rw_other))):
        copy = rcopy(src, dst, p_s.at[i], p_r.at[i], mate, x)
        copy.start()
        sends.append(copy)

    own_w = [
        pltpu.make_async_copy(
            w_cols(pl.ds(0, DIN), part, xx), wx.at[slot, :, pl.ds(part * COL, COL)], loc.at[0]
        )
        for xx, slot in ((x, across), (across, x))
        for part in range(2)
    ]

    def inside(h, _):
        cols = pl.ds(pl.multiple_of(h * DH, DH), DH)
        qh, kh, vh, doh = q_ref[:, cols], k_ref[:, cols], v_ref[:, cols], do_ref[:, cols]
        row = lax.broadcasted_iota(jnp.int32, (TOK, TOK), 0)
        col = lax.broadcasted_iota(jnp.int32, (TOK, TOK), 1)
        first = jnp.where(row >= col, mm(doh, vh, 1, 1), 0.0).astype(BF16)
        intra[0, :, cols] = mm(first, kh, 1, 0)
        third = jnp.where(row <= col, mm(vh, doh, 1, 1), 0.0).astype(BF16)
        intra[1, :, cols] = mm(third, qh, 1, 0)
        middle = jnp.where(row <= col, mm(kh, qh, 1, 1), 0.0).astype(BF16)
        intra[2, :, cols] = mm(middle, doh, 1, 0)
        return 0

    lax.fori_loop(0, HEADS // 2, inside, 0)

    forward = c == 0
    drains.append((own_states.at[most], a_s))

    def sum_of(u):
        total = got_states[0, part_of(u), :].astype(F32)
        for p in range(1, NM):
            total = total + got_states[p, part_of(u), :].astype(F32)
        return total

    def step_b(u):
        ref = got_states.at[most, part_of(u)]
        rcopy(ref, ref, a_s, a_r.at[u], mate, x).wait_recv()
        z_own[part_of(u), :] = sum_of(u).astype(BF16)
        for d in range(1, NZ):

            @pl.when(forward == (z + d < NZ))
            def _():
                rcopy(
                    z_own.at[part_of(u)], z_totals.at[z, part_of(u)],
                    b_s.at[d], b_r.at[u, d], lax.rem(z + d, NZ) * NM + m, x,
                ).start()

    step_b(0)
    step_b(1)

    for copy in own_w:
        copy.start()
    lax.fori_loop(HEADS // 2, HEADS, inside, 0)

    def weigh(src, weights, lanes):
        def one(q, _):
            yy = lax.rem(q, NY)
            zz = q // NY
            block = src[pl.ds(pl.multiple_of(q * RB, RB), RB), :].astype(F32)
            for e in range(2):
                value = (block * weights[e : e + 1, :]).astype(BF16)
                wy[yy, pl.ds(pl.multiple_of(e * NZ * RB + zz * RB, RB), RB), lanes] = value
                value = (block * weights[2 + e : 3 + e, :]).astype(BF16)
                wz[zz, pl.ds(pl.multiple_of(e * NY * RB + yy * RB, RB), RB), lanes] = value
            return 0

        lax.fori_loop(0, NY * NZ, one, 0)

    weigh(in_own, rw_own, pl.ds(0, TOK))

    share_weights()
    def step_c(u):
        rows = part_of(u)
        base[...] = jnp.zeros_like(base)
        for d in range(1, NZ):
            source = lax.rem(z + NZ - d, NZ)

            @pl.when(forward == (z >= d))
            def _():
                ref = z_totals.at[source, rows]
                rcopy(ref, ref, b_s.at[d], b_r.at[u, d], source * NM + m, x).wait_recv()
                base[...] += ref[...].astype(F32)

        start = base[...]
        before = jnp.zeros_like(start)
        total = sum_of(u)
        for p in range(NM):
            piece = got_states[p, rows, :].astype(F32)
            back_states[p, rows, :] = (start + jnp.where(forward, before, total - before - piece)).astype(BF16)
            before = before + piece
        for d in range(1, NM):
            p = lax.rem(m + d, NM)
            rcopy(back_states.at[p, rows], states.at[m, rows], c_s, c_r.at[u], z * NM + p, x).start()

    step_c(0)
    step_c(1)
    states[m] = back_states[m]

    rcopy(in_own, in_other, p_s.at[0], p_r.at[0], mate, x).wait_recv()
    rcopy(rw_own, rw_other, p_s.at[1], p_r.at[1], mate, x).wait_recv()
    weigh(in_other, rw_other, pl.ds(TOK, TOK))

    for u in range(2):
        ref = states.at[most, part_of(u)]
        rcopy(ref, ref, c_s, c_r.at[u], mate, x).wait_recv()
    drains.append((back_states.at[most], c_s))

    for h in range(HEADS):
        cols = slice(h * DH, (h + 1) * DH)
        late = states[2 * h + 1]
        grads[0, :, cols] = (intra[1, :, cols] + mm(v_ref[:, cols], late, 1, 1)).astype(BF16)
        grads[1, :, cols] = (intra[2, :, cols] + mm(k_ref[:, cols], late, 1, 0)).astype(BF16)
    copy = rcopy(grads.at[1 - c], other, p_s.at[2], p_r.at[2], mate, x)
    copy.start()
    sends.append(copy)

    def tokens(part):
        return pl.ds(part * (TOK // 2), TOK // 2)

    for part in range(2):
        rcopy(grads.at[:, tokens(part)], relay.at[:, tokens(part)], k_s, k_r.at[0, part], s, toward).start()
    drains.append((wx.at[0], k_s))

    def pass_on(part):
        ref = relay.at[:, tokens(part)]
        rcopy(ref, ref, k_s, k_r.at[0, part], s, toward).wait_recv()
        rcopy(ref, far_grads.at[:, tokens(part)], k_s, k_r.at[1, part], s, toward).start()

    for h in range(HEADS):
        cols = slice(h * DH, (h + 1) * DH)
        gq_buf[:, cols] = (intra[0, :, cols] + mm(do_ref[:, cols], states[2 * h], 1, 1)).astype(BF16)
    outs = [
        pltpu.make_async_copy(gq_buf, gq_out, loc.at[1]),
        pltpu.make_async_copy(grads.at[0], gk_out, loc.at[2]),
        pltpu.make_async_copy(grads.at[1], gv_out, loc.at[3]),
    ]
    for copy in outs:
        copy.start()

    def scale_of(e, rows):
        return jnp.sum(jnp.where(lane[rows] == e, rw_full[rows, :], 0.0), axis=1, keepdims=True)

    def project(e, slot, fresh, first, last):
        scale = scale_of(e, slice(0, TOK))

        def one(j, _):
            rows = pl.ds(pl.multiple_of(j * (DIN // NX), DIN // NX), DIN // NX)
            value = mm(grads[0], wx[slot, rows, 0:COL], 1, 1) + mm(grads[1], wx[slot, rows, COL : 2 * COL], 1, 1)
            value = scale * value
            ig_acc[j] = value if fresh else ig_acc[j] + value
            return 0

        lax.fori_loop(first, last, one, 0)


    rcopy(grads.at[0], other, p_s.at[2], p_r.at[2], mate, x).wait_recv()

    def dot_y(d):
        yy = lax.rem(y + d + NY, NY)
        for part in range(2):
            rows = pl.ds(part * 256, 256)
            value = mm(wy[yy, rows, 0:TOK], grads[c], 1, 0) + mm(wy[yy, rows, TOK : 2 * TOK], other[...], 1, 0)
            value = value.astype(BF16)
            py[0, yy, rows, :] = value[:, : COL // 2]
            py[1, yy, rows, :] = value[:, COL // 2 :]

    def dot_z(d):
        zz = lax.rem(z + d + NZ, NZ)
        value = mm(wz[zz, :, 0:TOK], grads[c], 1, 0) + mm(wz[zz, :, TOK : 2 * TOK], other[...], 1, 0)
        value = value.astype(BF16)
        pz[0, zz] = value[:, : COL // 2]
        pz[1, zz] = value[:, COL // 2 :]

    def rows_at(ref, u, offset):
        return ref.at[u, pl.ds(pl.multiple_of(offset, RB), RB)]

    ring_y1 = [
        ring(NY, y, at_y, lambda e, d, u=u: py.at[u, d, pl.ds(e * NZ * RB, NZ * RB)], y1.at[u], y1_s.at[u], y1_r.at[u], drains)
        for u in range(2)
    ]
    ring_z1 = [
        ring(NZ, z, at_z, lambda e, d, u=u: pz.at[u, d, pl.ds(e * NY * RB, NY * RB)], z1.at[u], z1_s.at[u], z1_r.at[u], drains)
        for u in range(2)
    ]
    ring_z2 = [
        ring(NZ, z, at_z, lambda e, d, u=u: rows_at(ry, u, e * NZ * RB + d * RB), z2.at[u], z2_s.at[u], z2_r.at[u], drains)
        for u in range(2)
    ]
    ring_y2 = [
        ring(NY, y, at_y, lambda e, d, u=u: rows_at(rz, u, e * NY * RB + d * RB), y2.at[u], y2_s.at[u], y2_r.at[u], drains)
        for u in range(2)
    ]
    ring_x = [
        ring(
            NX, x, at_x,
            lambda e, d, u=u: ig_send.at[d, pl.ds(u * (TOK // 2) + e * (TOK // 4), TOK // 4)],
            xr.at[u], x_s.at[u], x_r.at[u], drains,
        )
        for u in range(2)
    ]

    def y1_done(u):
        for e in range(2):
            ry[u, pl.ds(e * NZ * RB, NZ * RB), :] = step(ring_y1[u]).astype(BF16)
        step(ring_z2[u], 2)

    def z1_done(u):
        for e in range(2):
            rz[u, pl.ds(e * NY * RB, NY * RB), :] = step(ring_z1[u]).astype(BF16)
        step(ring_y2[u], 2)

    def hand_over(way, e):
        ref = wx.at[e, half]
        rcopy(ref, ref, h_s, h_r.at[way], mate, x).start()

    drains.append((wx.at[0], h_s))

    def handed(way, e):
        ref = wx.at[e, pl.ds(pl.multiple_of((1 - c) * (DIN // 2), DIN // 2), DIN // 2)]
        rcopy(ref, ref, h_s, h_r.at[way], mate, x).wait_recv()

    def last_project(u):
        ref = far_grads.at[:, tokens(u)]
        rcopy(ref, ref, k_s, k_r.at[1, u], s, toward).wait_recv()
        scale = scale_of(x, slice(u * (TOK // 2), (u + 1) * (TOK // 2)))

        def one(j, _):
            rows = pl.ds(pl.multiple_of(j * (DIN // NX), DIN // NX), DIN // NX)
            value = mm(far_grads[0, tokens(u), :], wx[x, rows, 0:COL], 1, 1) + mm(
                far_grads[1, tokens(u), :], wx[x, rows, COL : 2 * COL], 1, 1
            )
            ig_send[j, tokens(u), :] = (ig_acc[j, tokens(u), :] + scale * value).astype(BF16)
            return 0

        lax.fori_loop(0, NX, one, 0)
        step(ring_x[u], 2)

    def finish(e, u, total):
        fin[u, e] = total
        for core in range(2):
            src = fin.at[u, e, pl.ds(core * (RB // 2), RB // 2)]
            first = c * (NX * COL) + x * COL + u * (COL // 2)
            dst = wg_buf.at[:, pl.ds(pl.multiple_of(first, COL // 2), COL // 2)]
            here = jnp.logical_and(x == e, c == core)

            @pl.when(jnp.logical_not(here))
            def _():
                rcopy(src, dst, f_s, f_r, s - c + core, e).start()

            @pl.when(here)
            def _():
                dst[...] = src[...]

    def finish_y(u):
        for e in range(2):
            finish(2 + e, u, step(ring_y2[u]))

    def finish_z(u):
        for e in range(2):
            finish(e, u, step(ring_z2[u]))

    def ig_done(u):
        for e in range(2):
            ig_buf[pl.ds(u * (TOK // 2) + e * (TOK // 4), TOK // 4), :] = step(ring_x[u]).astype(BF16)

    dot_y(2)
    step(ring_y1[0])
    dot_z(4)
    step(ring_z1[0])
    step(ring_z1[1])
    dot_y(1)
    dot_y(-1)
    step(ring_y1[0])
    dot_z(3)
    dot_z(-3)
    step(ring_z1[0])
    step(ring_z1[1])
    all_weights()
    hand_over(0, left)
    hand_over(1, right)
    dot_z(2)
    dot_z(-2)
    dot_y(0)
    pltpu.make_async_copy(wx.at[pl.ds(0, 2)], wx.at[pl.ds(0, 2)], loc.at[0]).wait()
    project(x, across, True, 0, 2)
    step(ring_y1[0])
    step(ring_y1[1], 2)
    project(x, across, True, 2, 4)
    step(ring_z1[0])
    pass_on(0)
    dot_z(1)
    dot_z(-1)
    step(ring_z1[1])
    dot_z(0)
    handed(0, left)
    project(left, left, False, 0, 4)
    step(ring_z1[0])
    step(ring_y1[1])
    pass_on(1)
    handed(1, right)
    project(right, right, False, 0, 2)
    step(ring_z1[1])
    step(ring_z1[0])
    project(right, right, False, 2, 4)
    y1_done(0)
    y1_done(1)
    step(ring_z1[1])
    z1_done(0)
    step(ring_z2[0])
    z1_done(1)
    step(ring_z2[1])
    last_project(0)
    step(ring_z2[0])
    step(ring_y2[0])
    step(ring_z2[1])
    step(ring_y2[1])
    last_project(1)
    step(ring_z2[0])
    step(ring_z2[1])
    finish_y(0)
    step(ring_x[0])
    finish_y(1)
    finish_z(0)
    finish_z(1)
    step(ring_x[1])
    ig_done(0)
    arriving = wg_buf.at[:, pl.ds(0, 2 * (2 * NX - 1) * (COL // 2))]
    rcopy(arriving, arriving, f_s, f_r, mate, x).wait_recv()
    drains.append((arriving, f_s))
    outs.append(pltpu.make_async_copy(wg_buf, wg_out, loc.at[4]))
    outs[-1].start()
    ig_done(1)
    outs.append(pltpu.make_async_copy(ig_buf, ig_out, loc.at[5]))
    outs[-1].start()

    for copy in sends:
        copy.wait_send()
    for d in range(1, NZ):

        @pl.when(forward == (z + d < NZ))
        def _():
            rcopy(z_own, z_own, b_s.at[d], b_r.at[0, d], mate, x).wait_send()

    for ref, sem in drains:
        rcopy(ref, ref, sem, a_r.at[0], mate, x).wait_send()
    for copy in outs:
        copy.wait()


def write_out(*refs):
    sems = refs[10]
    copies = [pltpu.make_async_copy(refs[i], refs[5 + i], sems.at[i]) for i in range(5)]
    for copy in copies:
        copy.start()
    for copy in copies:
        copy.wait()


def per_device(query_in, key_in, value_in, out_grad, inputs, expert_ids, route_gates, expert_weight):
    vmem = pl.BlockSpec(memory_space=pltpu.VMEM)
    anywhere = pl.BlockSpec(memory_space=pl.ANY)
    dma = pltpu.SemaphoreType.DMA

    def v(shape, dtype=BF16):
        return pltpu.VMEM(shape, dtype)

    scratch = [
        v((TOK, COL)), v((TOK, COL)), v((TOK, COL)), v((TOK, COL)), v((TOK, DIN)), v((2, TOK), jnp.int32), v((2, TOK), F32),
        v((NM, DH, DH)), v((NM, DH, DH)), v((NZ, DH, DH)), v((DH, DH)), v((NM, DH, DH)), v((NM, DH, DH)),
        v((DH // 2, DH), F32),
        v((3, TOK, COL), F32), v((2, TOK, COL)), v((TOK, COL)), v((TOK, COL)),
        v((DIN, TOK)), v((DIN, TOK)), v((TOK, DH), F32), v((8, TOK), F32), v((8, TOK), F32),
        v((NY, 2 * NZ * RB, 2 * TOK)), v((NZ, 2 * NY * RB, 2 * TOK)),
        v((2, NY, 2 * NZ * RB, COL // 2)), v((2, NZ, 2 * NY * RB, COL // 2)),
        v((2, NY - 1, 2, NZ * RB, COL // 2)), v((2, NZ - 1, 2, RB, COL // 2)),
        v((2, NZ - 1, 2, NY * RB, COL // 2)), v((2, NY - 1, 2, RB, COL // 2)),
        v((2, NX - 1, 2, TOK // 4, DIN // NX)),
        v((2, 2 * NZ * RB, COL // 2)), v((2, 2 * NY * RB, COL // 2)),
        v((2, NX, RB, COL // 2), F32), v((RB // 2, 2 * NX * COL), F32),
        v((NX, DIN, 2 * COL)), v((2, TOK, COL)), v((2, TOK, COL)),
        v((NX, TOK, DIN // NX), F32), v((NX, TOK, DIN // NX)), v((TOK, DIN // NX)),
        dma(()), dma((2,)), dma((NZ,)), dma((2, NZ)), dma(()), dma((2,)),
        dma((2,)), dma((2, NY - 1)), dma((2,)), dma((2, NZ - 1)),
        dma((2,)), dma((2, NZ - 1)), dma((2,)), dma((2, NY - 1)),
        dma((2,)), dma((2, NX - 1)),
        dma(()), dma(()), dma(()), dma(()), dma((3,)), dma(()), dma((2,)),
        dma(()), dma((2, 2)), dma((3,)), dma((3,)), dma((6,)), dma((7,)),
    ]
    gq, gk, gv, ig, wg = pl.pallas_call(
        kernel,
        out_shape=(
            pltpu.VMEM((TOK, COL), BF16),
            pltpu.VMEM((TOK, COL), BF16),
            pltpu.VMEM((TOK, COL), BF16),
            pltpu.VMEM((TOK, DIN // NX), BF16),
            pltpu.VMEM((RB // 2, 2 * NX * COL), F32),
        ),
        in_specs=[anywhere] * 8,
        out_specs=(anywhere,) * 5,
        scratch_shapes=scratch,
        compiler_params=pltpu.CompilerParams(
            collective_id=0, has_side_effects=True, vmem_limit_bytes=56 * 1024 * 1024
        ),
    )(query_in, key_in, value_in, out_grad, inputs, expert_ids.T, route_gates.T, expert_weight)
    gq, gk, gv, ig, wg = pl.pallas_call(
        write_out,
        out_shape=tuple(jax.ShapeDtypeStruct(a.shape, a.dtype) for a in (gq, gk, gv, ig, wg)),
        in_specs=[vmem] * 5,
        out_specs=(anywhere,) * 5,
        scratch_shapes=[dma((5,))],
    )(*(pltpu.with_memory_space_constraint(a, pltpu.VMEM) for a in (gq, gk, gv, ig, wg)))
    return gq, gk, gv, ig, wg[None]


def solution(mesh):
    return jax.shard_map(
        per_device,
        mesh=mesh,
        in_specs=(
            P("seq", "exp"), P("seq", "exp"), P("seq", "exp"), P("seq", "exp"),
            P("seq", None), P("seq", None), P("seq", None), P("exp", None, None),
        ),
        out_specs=(
            P("seq", "exp"), P("seq", "exp"), P("seq", "exp"), P("seq", "exp"), P("exp", "seq", None),
        ),
        check_vma=False,
    )
```

```python
import jax
import jax.numpy as jnp
from jax import lax
from jax.experimental import pallas as pl
from jax.experimental.pallas import tpu as pltpu
from jax.sharding import PartitionSpec as P

MESH = pl.DeviceIdType.MESH
F32 = jnp.float32
BF16 = jnp.bfloat16
NX = 4
NY = 4
NZ = 8
NM = 2 * NY
DH = 128
HEADS = 4
TOK = 512
COL = 512
DIN = 1024
RB = 32
SHARE = 64


def mm(a, b, ca, cb):
    return lax.dot_general(a, b, (((ca,), (cb,)), ((), ())), preferred_element_type=F32)


def rcopy(src, dst, ssem, rsem, seq, exp):
    return pltpu.make_async_remote_copy(
        src_ref=src,
        dst_ref=dst,
        send_sem=ssem,
        recv_sem=rsem,
        device_id={"seq": seq, "exp": exp},
        device_id_type=MESH,
    )


def ring(count, place, neighbour, block, slots, ssem, rsem, drains):
    pairs = []
    for far in (True, False):
        hops = count // 2 if far else (count - 1) // 2
        pairs.append((hops, [(e, 1 if (e == 0) == far else -1) for e in range(2)]))
    drains.append((slots, ssem))

    def index(pair, hop):
        return hop + (0 if pair == 0 else pairs[0][0])

    def go(src, pair, i, hop):
        seq, exp = neighbour(pairs[pair][1][i][1])
        at = index(pair, hop)
        rcopy(src, slots.at[at, i], ssem, rsem.at[at], seq, exp).start()

    def arrived(pair, hop):
        seq, exp = neighbour(1)
        at = index(pair, hop)
        rcopy(slots.at[at], slots.at[at], ssem, rsem.at[at], seq, exp).wait_recv()

    for hop in range(count // 2):
        for pair, (hops, flows) in enumerate(pairs):
            if hop >= hops:
                continue
            if hop:
                arrived(pair, hop - 1)
            for i, (e, sign) in enumerate(flows):
                dest = lax.rem(place + sign * (hops - hop) + 2 * count, count)
                if hop:
                    ref = slots.at[index(pair, hop - 1), i]
                    ref[...] = (ref[...].astype(F32) + block(e, dest)[...].astype(F32)).astype(BF16)
                    go(ref, pair, i, hop)
                else:
                    go(block(e, dest), pair, i, 0)
            if not hop:
                yield None
        if hop:
            yield None
    for pair, (hops, _) in enumerate(pairs):
        arrived(pair, hops - 1)
    for e in range(2):
        total = block(e, place)[...].astype(F32)
        for pair, (hops, _) in enumerate(pairs):
            total = total + slots[index(pair, hops - 1), e].astype(F32)
        yield total


def step(generator, times=1):
    for _ in range(times):
        value = next(generator)
    return value


def kernel(
    q_in, k_in, v_in, do_in, inp_in, ids_in, gates_in, w_ref,
    gq_out, gk_out, gv_out, ig_out, wg_out,
    q_ref, k_ref, v_ref, do_ref, inp_ref, ids_ref, gates_ref,
    own_states, got_states, z_totals, z_own, back_states, states, base,
    intra, grads, other, gq_buf, in_own, in_other, rw_full, rw_own, rw_other,
    wy, wz, py, pz, y1, z2, z1, y2, xr, ry, rz, fin, wg_got, wg_buf,
    wx, relay, far_grads, ig_acc, ig_send, ig_buf,
    a_s, a_r, b_s, b_r, c_s, c_r, y1_s, y1_r, z2_s, z2_r, z1_s, z1_r, y2_s, y2_r, x_s, x_r,
    f_s, f_r, w_s, w_s2, w_r, h_s, h_r, k_s, k_r, p_s, p_r, loc, load,
):
    s = lax.axis_index("seq")
    x = lax.axis_index("exp")
    m = lax.rem(s, NM)
    z = s // NM
    c = lax.rem(s, 2)
    y = m // 2
    mate = s + 1 - 2 * c
    sends, drains = [], []
    most = pl.ds(0, NM - 1)

    def at_y(sign):
        return z * NM + lax.rem(y + sign + NY, NY) * 2 + c, x

    def at_z(sign):
        return lax.rem(z + sign + NZ, NZ) * NM + m, x

    def at_x(sign):
        return s, lax.rem(x + sign + NX, NX)

    barrier = pltpu.get_barrier_semaphore()
    peers = 0
    for d in range(1, NM):
        pl.semaphore_signal(barrier, inc=1, device_id={"seq": z * NM + lax.rem(m + d, NM), "exp": x}, device_id_type=MESH)
        peers += 1
    for d in range(1, NZ):
        pl.semaphore_signal(barrier, inc=1, device_id={"seq": lax.rem(z + d, NZ) * NM + m, "exp": x}, device_id_type=MESH)
        peers += 1
    for d in range(1, NX):
        for other_core in range(2):
            pl.semaphore_signal(barrier, inc=1, device_id={"seq": s - c + other_core, "exp": lax.rem(x + d, NX)}, device_id_type=MESH)
            peers += 1

    pairs = (
        (k_in, k_ref), (v_in, v_ref), (q_in, q_ref), (do_in, do_ref),
        (ids_in, ids_ref), (gates_in, gates_ref), (inp_in, inp_ref),
    )
    loads = [pltpu.make_async_copy(src, dst, load.at[i]) for i, (src, dst) in enumerate(pairs)]
    for copy in loads[:4]:
        copy.start()

    for copy in loads[:2]:
        copy.wait()

    def own_kv(h, _):
        cols = pl.ds(pl.multiple_of(h * DH, DH), DH)
        own_states[2 * h] = mm(k_ref[:, cols], v_ref[:, cols], 0, 0).astype(BF16)
        return 0

    lax.fori_loop(0, HEADS, own_kv, 0)
    for copy in loads[2:4]:
        copy.wait()
    for copy in loads[4:]:
        copy.start()

    def own_qo(h, _):
        cols = pl.ds(pl.multiple_of(h * DH, DH), DH)
        own_states[2 * h + 1] = mm(q_ref[:, cols], do_ref[:, cols], 0, 0).astype(BF16)
        return 0

    lax.fori_loop(0, HEADS, own_qo, 0)

    pl.semaphore_wait(barrier, peers)

    def part_of(u):
        return pl.ds(u * (DH // 2), DH // 2)

    for u in range(2):
        for d in range(1, NM):
            p = lax.rem(m + d, NM)
            rcopy(own_states.at[p, part_of(u)], got_states.at[m, part_of(u)], a_s, a_r.at[u], z * NM + p, x).start()
    got_states[m] = own_states[m]

    def w_cols(rows, part, xx):
        return w_ref.at[0, rows, pl.ds(pl.multiple_of(part * (NX * COL) + xx * COL, COL), COL)]

    start_row = c * (DIN // 2)
    half = pl.ds(pl.multiple_of(start_row, DIN // 2), DIN // 2)
    left, right = lax.rem(x + 3, NX), lax.rem(x + 1, NX)
    toward = lax.rem(x + 1 + 2 * c, NX)
    across = lax.rem(x + 2, NX)
    odd = lax.rem(z, 2)

    def w_rows(offset, count):
        return pl.ds(pl.multiple_of(start_row + offset, 16), count)

    alone = DIN // 2 - 4 * SHARE
    shared = w_rows(alone + 2 * SHARE * odd, 2 * SHARE)
    for rows, sem in ((shared, 0), (w_rows(0, alone), 1)):
        for to in (right, left):
            for part in range(2):
                rcopy(w_cols(rows, part, to), wx.at[x, rows, pl.ds(part * COL, COL)], w_s, w_r.at[sem], s, to).start()
    drains.append((wx.at[0, pl.ds(0, DIN - 4 * SHARE)], w_s))

    def share_weights():
        ref = wx.at[0, pl.ds(0, 4 * SHARE)]
        rcopy(ref, ref, w_s, w_r.at[0], s, toward).wait_recv()
        for e in (left, right):
            for i, sign in ((0, 1 - 2 * odd), (1, 2 * odd - 1)):
                ref = wx.at[e, w_rows(alone + 2 * SHARE * odd + SHARE * i, SHARE)]
                seq, exp = at_z(sign)
                rcopy(ref, ref, w_s2, w_r.at[2], seq, exp).start()
        drains.append((wx.at[0, pl.ds(0, 4 * SHARE)], w_s2))

    def all_weights():
        ref = wx.at[0, pl.ds(0, 2 * alone)]
        rcopy(ref, ref, w_s, w_r.at[1], s, toward).wait_recv()
        ref = wx.at[0, pl.ds(0, 4 * SHARE)]
        rcopy(ref, ref, w_s, w_r.at[2], s, toward).wait_recv()

    for copy in loads[4:]:
        copy.wait()
    lane = lax.broadcasted_iota(jnp.int32, (TOK, DH), 1)
    expert = lax.broadcasted_iota(jnp.int32, (DH, TOK), 0)
    rw = jnp.where(ids_ref[0:1, :] == expert, gates_ref[0:1, :], 0.0) + jnp.where(
        ids_ref[1:2, :] == expert, gates_ref[1:2, :], 0.0
    )
    rw_full[...] = rw.T
    rw_own[...] = rw[0:8, :]

    def turn(j, _):
        cols = pl.ds(pl.multiple_of(j * DH, DH), DH)
        in_own[cols, :] = inp_ref[:, cols].astype(F32).T.astype(BF16)
        return 0

    lax.fori_loop(0, DIN // DH, turn, 0)
    for i, (src, dst) in enumerate(((in_own, in_other), (rw_own, rw_other))):
        copy = rcopy(src, dst, p_s.at[i], p_r.at[i], mate, x)
        copy.start()
        sends.append(copy)

    own_w = [
        pltpu.make_async_copy(
            w_cols(pl.ds(0, DIN), part, xx), wx.at[slot, :, pl.ds(part * COL, COL)], loc.at[0]
        )
        for xx, slot in ((x, across), (across, x))
        for part in range(2)
    ]

    def inside(h, _):
        cols = pl.ds(pl.multiple_of(h * DH, DH), DH)
        qh, kh, vh, doh = q_ref[:, cols], k_ref[:, cols], v_ref[:, cols], do_ref[:, cols]
        row = lax.broadcasted_iota(jnp.int32, (TOK, TOK), 0)
        col = lax.broadcasted_iota(jnp.int32, (TOK, TOK), 1)
        first = jnp.where(row >= col, mm(doh, vh, 1, 1), 0.0).astype(BF16)
        intra[0, :, cols] = mm(first, kh, 1, 0)
        third = jnp.where(row <= col, mm(vh, doh, 1, 1), 0.0).astype(BF16)
        intra[1, :, cols] = mm(third, qh, 1, 0)
        middle = jnp.where(row <= col, mm(kh, qh, 1, 1), 0.0).astype(BF16)
        intra[2, :, cols] = mm(middle, doh, 1, 0)
        return 0

    lax.fori_loop(0, HEADS // 2, inside, 0)

    forward = c == 0
    drains.append((own_states.at[most], a_s))

    def sum_of(u):
        total = got_states[0, part_of(u), :].astype(F32)
        for p in range(1, NM):
            total = total + got_states[p, part_of(u), :].astype(F32)
        return total

    def step_b(u):
        ref = got_states.at[most, part_of(u)]
        rcopy(ref, ref, a_s, a_r.at[u], mate, x).wait_recv()
        z_own[part_of(u), :] = sum_of(u).astype(BF16)
        for d in range(1, NZ):

            @pl.when(forward == (z + d < NZ))
            def _():
                rcopy(
                    z_own.at[part_of(u)], z_totals.at[z, part_of(u)],
                    b_s.at[d], b_r.at[u, d], lax.rem(z + d, NZ) * NM + m, x,
                ).start()

    step_b(0)
    step_b(1)

    for copy in own_w:
        copy.start()
    lax.fori_loop(HEADS // 2, HEADS, inside, 0)

    def weigh(src, weights, lanes):
        def one(q, _):
            yy = lax.rem(q, NY)
            zz = q // NY
            block = src[pl.ds(pl.multiple_of(q * RB, RB), RB), :].astype(F32)
            for e in range(2):
                value = (block * weights[e : e + 1, :]).astype(BF16)
                wy[yy, pl.ds(pl.multiple_of(e * NZ * RB + zz * RB, RB), RB), lanes] = value
                value = (block * weights[2 + e : 3 + e, :]).astype(BF16)
                wz[zz, pl.ds(pl.multiple_of(e * NY * RB + yy * RB, RB), RB), lanes] = value
            return 0

        lax.fori_loop(0, NY * NZ, one, 0)

    weigh(in_own, rw_own, pl.ds(0, TOK))

    def step_c(u):
        rows = part_of(u)
        base[...] = jnp.zeros_like(base)
        for d in range(1, NZ):
            source = lax.rem(z + NZ - d, NZ)

            @pl.when(forward == (z >= d))
            def _():
                ref = z_totals.at[source, rows]
                rcopy(ref, ref, b_s.at[d], b_r.at[u, d], source * NM + m, x).wait_recv()
                base[...] += ref[...].astype(F32)

        start = base[...]
        before = jnp.zeros_like(start)
        total = sum_of(u)
        for p in range(NM):
            piece = got_states[p, rows, :].astype(F32)
            back_states[p, rows, :] = (start + jnp.where(forward, before, total - before - piece)).astype(BF16)
            before = before + piece
        for d in range(1, NM):
            p = lax.rem(m + d, NM)
            rcopy(back_states.at[p, rows], states.at[m, rows], c_s, c_r.at[u], z * NM + p, x).start()

    step_c(0)
    step_c(1)
    states[m] = back_states[m]
    share_weights()

    rcopy(in_own, in_other, p_s.at[0], p_r.at[0], mate, x).wait_recv()
    rcopy(rw_own, rw_other, p_s.at[1], p_r.at[1], mate, x).wait_recv()
    weigh(in_other, rw_other, pl.ds(TOK, TOK))

    for u in range(2):
        ref = states.at[most, part_of(u)]
        rcopy(ref, ref, c_s, c_r.at[u], mate, x).wait_recv()
    drains.append((back_states.at[most], c_s))

    for h in range(HEADS):
        cols = slice(h * DH, (h + 1) * DH)
        late = states[2 * h + 1]
        grads[0, :, cols] = (intra[1, :, cols] + mm(v_ref[:, cols], late, 1, 1)).astype(BF16)
        grads[1, :, cols] = (intra[2, :, cols] + mm(k_ref[:, cols], late, 1, 0)).astype(BF16)
    copy = rcopy(grads.at[1 - c], other, p_s.at[2], p_r.at[2], mate, x)
    copy.start()
    sends.append(copy)

    def tokens(part):
        return pl.ds(part * (TOK // 2), TOK // 2)

    for part in range(2):
        rcopy(grads.at[:, tokens(part)], relay.at[:, tokens(part)], k_s, k_r.at[0, part], s, toward).start()
    drains.append((wx.at[0], k_s))

    def pass_on(part):
        ref = relay.at[:, tokens(part)]
        rcopy(ref, ref, k_s, k_r.at[0, part], s, toward).wait_recv()
        rcopy(ref, far_grads.at[:, tokens(part)], k_s, k_r.at[1, part], s, toward).start()

    def scale_of(e, rows):
        return jnp.sum(jnp.where(lane[rows] == e, rw_full[rows, :], 0.0), axis=1, keepdims=True)

    def project(e, slot, fresh, first, last):
        scale = scale_of(e, slice(0, TOK))

        def one(j, _):
            rows = pl.ds(pl.multiple_of(j * (DIN // NX), DIN // NX), DIN // NX)
            value = mm(grads[0], wx[slot, rows, 0:COL], 1, 1) + mm(grads[1], wx[slot, rows, COL : 2 * COL], 1, 1)
            value = scale * value
            ig_acc[j] = value if fresh else ig_acc[j] + value
            return 0

        lax.fori_loop(first, last, one, 0)


    pltpu.make_async_copy(wx.at[pl.ds(0, 2)], wx.at[pl.ds(0, 2)], loc.at[0]).wait()
    project(x, across, True, 0, 2)
    rcopy(grads.at[0], other, p_s.at[2], p_r.at[2], mate, x).wait_recv()

    def dot_y(d, u):
        yy = lax.rem(y + d + NY, NY)
        cols = slice(u * (COL // 2), (u + 1) * (COL // 2))
        for part in range(2):
            rows = pl.ds(part * 256, 256)
            value = mm(wy[yy, rows, 0:TOK], grads[c, :, cols], 1, 0) + mm(wy[yy, rows, TOK : 2 * TOK], other[:, cols], 1, 0)
            py[u, yy, rows, :] = value.astype(BF16)

    def dot_z(d, u):
        zz = lax.rem(z + d + NZ, NZ)
        cols = slice(u * (COL // 2), (u + 1) * (COL // 2))
        value = mm(wz[zz, :, 0:TOK], grads[c, :, cols], 1, 0) + mm(wz[zz, :, TOK : 2 * TOK], other[:, cols], 1, 0)
        pz[u, zz] = value.astype(BF16)

    ring_y1 = [
        ring(NY, y, at_y, lambda e, d, u=u: py.at[u, d, pl.ds(e * NZ * RB, NZ * RB)], y1.at[u], y1_s.at[u], y1_r.at[u], drains)
        for u in range(2)
    ]
    ring_z1 = [
        ring(NZ, z, at_z, lambda e, d, u=u: pz.at[u, d, pl.ds(e * NY * RB, NY * RB)], z1.at[u], z1_s.at[u], z1_r.at[u], drains)
        for u in range(2)
    ]
    ring_z2 = ring(
        NZ, z, at_z,
        lambda e, d: ry.at[pl.ds(pl.multiple_of(e * NZ * RB + d * RB, RB), RB)],
        z2, z2_s, z2_r, drains,
    )
    ring_y2 = ring(
        NY, y, at_y,
        lambda e, d: rz.at[pl.ds(pl.multiple_of(e * NY * RB + d * RB, RB), RB)],
        y2, y2_s, y2_r, drains,
    )
    ring_x = [
        ring(
            NX, x, at_x,
            lambda e, d, u=u: ig_send.at[d, pl.ds(u * (TOK // 2) + e * (TOK // 4), TOK // 4)],
            xr.at[u], x_s.at[u], x_r.at[u], drains,
        )
        for u in range(2)
    ]

    def y1_done(u):
        for e in range(2):
            ry[pl.ds(e * NZ * RB, NZ * RB), pl.ds(u * (COL // 2), COL // 2)] = step(ring_y1[u]).astype(BF16)

    def z1_done(u):
        for e in range(2):
            rz[pl.ds(e * NY * RB, NY * RB), pl.ds(u * (COL // 2), COL // 2)] = step(ring_z1[u]).astype(BF16)

    def hand_over(way, e):
        ref = wx.at[e, half]
        rcopy(ref, ref, h_s, h_r.at[way], mate, x).start()

    drains.append((wx.at[0], h_s))

    def handed(way, e):
        ref = wx.at[e, pl.ds(pl.multiple_of((1 - c) * (DIN // 2), DIN // 2), DIN // 2)]
        rcopy(ref, ref, h_s, h_r.at[way], mate, x).wait_recv()

    def last_project(u):
        ref = far_grads.at[:, tokens(u)]
        rcopy(ref, ref, k_s, k_r.at[1, u], s, toward).wait_recv()
        scale = scale_of(x, slice(u * (TOK // 2), (u + 1) * (TOK // 2)))

        def one(j, _):
            rows = pl.ds(pl.multiple_of(j * (DIN // NX), DIN // NX), DIN // NX)
            value = mm(far_grads[0, tokens(u), :], wx[x, rows, 0:COL], 1, 1) + mm(
                far_grads[1, tokens(u), :], wx[x, rows, COL : 2 * COL], 1, 1
            )
            ig_send[j, tokens(u), :] = (ig_acc[j, tokens(u), :] + scale * value).astype(BF16)
            return 0

        lax.fori_loop(0, NX, one, 0)
        step(ring_x[u], 2)

    def finish(e, total):
        fin[e] = total.astype(BF16)
        for core in range(2):
            src = fin.at[e, pl.ds(core * (RB // 2), RB // 2)]
            dst = wg_got.at[:, pl.ds(pl.multiple_of(c * (NX * COL) + x * COL, COL), COL)]
            here = jnp.logical_and(x == e, c == core)

            @pl.when(jnp.logical_not(here))
            def _():
                rcopy(src, dst, f_s, f_r, s - c + core, e).start()

            @pl.when(here)
            def _():
                dst[...] = src[...]

    def finish_y():
        for e in range(2):
            finish(2 + e, step(ring_y2))

    def finish_z():
        for e in range(2):
            finish(e, step(ring_z2))

    def ig_done(u):
        for e in range(2):
            ig_buf[pl.ds(u * (TOK // 2) + e * (TOK // 4), TOK // 4), :] = step(ring_x[u]).astype(BF16)

    dot_y(2, 0)
    step(ring_y1[0])
    dot_z(4, 0)
    step(ring_z1[0])
    dot_z(4, 1)
    step(ring_z1[1])
    dot_y(1, 0)
    dot_y(-1, 0)
    step(ring_y1[0])
    for u in range(2):
        dot_z(3, u)
        dot_z(-3, u)
        step(ring_z1[u])
    for h in range(HEADS):
        cols = slice(h * DH, (h + 1) * DH)
        gq_buf[:, cols] = (intra[0, :, cols] + mm(do_ref[:, cols], states[2 * h], 1, 1)).astype(BF16)
    outs = [
        pltpu.make_async_copy(gq_buf, gq_out, loc.at[1]),
        pltpu.make_async_copy(grads.at[0], gk_out, loc.at[2]),
        pltpu.make_async_copy(grads.at[1], gv_out, loc.at[3]),
    ]
    for copy in outs:
        copy.start()
    all_weights()
    hand_over(0, left)
    hand_over(1, right)
    dot_y(2, 1)
    dot_y(1, 1)
    dot_y(-1, 1)
    dot_z(2, 0)
    dot_z(-2, 0)
    step(ring_y1[0])
    step(ring_y1[1], 2)
    dot_z(2, 1)
    dot_z(-2, 1)
    dot_y(0, 0)
    step(ring_z1[0])
    project(x, across, True, 2, 4)
    step(ring_z1[1])
    pass_on(0)
    dot_y(0, 1)
    for d in (1, -1, 0):
        dot_z(d, 0)
        dot_z(d, 1)
    handed(0, left)
    project(left, left, False, 0, 2)
    step(ring_z1[0])
    project(left, left, False, 2, 4)
    step(ring_y1[1])
    pass_on(1)
    step(ring_z1[1])
    handed(1, right)
    project(right, right, False, 0, 2)
    step(ring_z1[0])
    project(right, right, False, 2, 4)
    y1_done(0)
    y1_done(1)
    step(ring_z2, 2)
    step(ring_z1[1])
    last_project(0)
    z1_done(0)
    step(ring_z2)
    z1_done(1)
    step(ring_y2, 2)
    step(ring_z2)
    last_project(1)
    step(ring_y2)
    step(ring_x[0])
    step(ring_z2)
    finish_y()
    finish_z()
    step(ring_x[1])
    ig_done(0)
    arriving = wg_got.at[:, pl.ds(0, (2 * NX - 1) * COL)]
    rcopy(arriving, arriving, f_s, f_r, mate, x).wait_recv()
    drains.append((arriving, f_s))
    wg_buf[...] = wg_got[...].astype(F32)
    outs.append(pltpu.make_async_copy(wg_buf, wg_out, loc.at[4]))
    outs[-1].start()
    ig_done(1)
    outs.append(pltpu.make_async_copy(ig_buf, ig_out, loc.at[5]))
    outs[-1].start()

    for copy in sends:
        copy.wait_send()
    for d in range(1, NZ):

        @pl.when(forward == (z + d < NZ))
        def _():
            rcopy(z_own, z_own, b_s.at[d], b_r.at[0, d], mate, x).wait_send()

    for ref, sem in drains:
        rcopy(ref, ref, sem, a_r.at[0], mate, x).wait_send()
    for copy in outs:
        copy.wait()


def write_out(*refs):
    sems = refs[10]
    copies = [pltpu.make_async_copy(refs[i], refs[5 + i], sems.at[i]) for i in range(5)]
    for copy in copies:
        copy.start()
    for copy in copies:
        copy.wait()


def per_device(query_in, key_in, value_in, out_grad, inputs, expert_ids, route_gates, expert_weight):
    vmem = pl.BlockSpec(memory_space=pltpu.VMEM)
    anywhere = pl.BlockSpec(memory_space=pl.ANY)
    dma = pltpu.SemaphoreType.DMA

    def v(shape, dtype=BF16):
        return pltpu.VMEM(shape, dtype)

    scratch = [
        v((TOK, COL)), v((TOK, COL)), v((TOK, COL)), v((TOK, COL)), v((TOK, DIN)), v((2, TOK), jnp.int32), v((2, TOK), F32),
        v((NM, DH, DH)), v((NM, DH, DH)), v((NZ, DH, DH)), v((DH, DH)), v((NM, DH, DH)), v((NM, DH, DH)),
        v((DH // 2, DH), F32),
        v((3, TOK, COL), F32), v((2, TOK, COL)), v((TOK, COL)), v((TOK, COL)),
        v((DIN, TOK)), v((DIN, TOK)), v((TOK, DH), F32), v((8, TOK), F32), v((8, TOK), F32),
        v((NY, 2 * NZ * RB, 2 * TOK)), v((NZ, 2 * NY * RB, 2 * TOK)),
        v((2, NY, 2 * NZ * RB, COL // 2)), v((2, NZ, 2 * NY * RB, COL // 2)),
        v((2, NY - 1, 2, NZ * RB, COL // 2)), v((NZ - 1, 2, RB, COL)),
        v((2, NZ - 1, 2, NY * RB, COL // 2)), v((NY - 1, 2, RB, COL)),
        v((2, NX - 1, 2, TOK // 4, DIN // NX)),
        v((2 * NZ * RB, COL)), v((2 * NY * RB, COL)),
        v((NX, RB, COL)), v((RB // 2, 2 * NX * COL)), v((RB // 2, 2 * NX * COL), F32),
        v((NX, DIN, 2 * COL)), v((2, TOK, COL)), v((2, TOK, COL)),
        v((NX, TOK, DIN // NX), F32), v((NX, TOK, DIN // NX)), v((TOK, DIN // NX)),
        dma(()), dma((2,)), dma((NZ,)), dma((2, NZ)), dma(()), dma((2,)),
        dma((2,)), dma((2, NY - 1)), dma(()), dma((NZ - 1,)),
        dma((2,)), dma((2, NZ - 1)), dma(()), dma((NY - 1,)),
        dma((2,)), dma((2, NX - 1)),
        dma(()), dma(()), dma(()), dma(()), dma((3,)), dma(()), dma((2,)),
        dma(()), dma((2, 2)), dma((3,)), dma((3,)), dma((6,)), dma((7,)),
    ]
    gq, gk, gv, ig, wg = pl.pallas_call(
        kernel,
        out_shape=(
            pltpu.VMEM((TOK, COL), BF16),
            pltpu.VMEM((TOK, COL), BF16),
            pltpu.VMEM((TOK, COL), BF16),
            pltpu.VMEM((TOK, DIN // NX), BF16),
            pltpu.VMEM((RB // 2, 2 * NX * COL), F32),
        ),
        in_specs=[anywhere] * 8,
        out_specs=(anywhere,) * 5,
        scratch_shapes=scratch,
        compiler_params=pltpu.CompilerParams(
            collective_id=0, has_side_effects=True, vmem_limit_bytes=56 * 1024 * 1024
        ),
    )(query_in, key_in, value_in, out_grad, inputs, expert_ids.T, route_gates.T, expert_weight)
    gq, gk, gv, ig, wg = pl.pallas_call(
        write_out,
        out_shape=tuple(jax.ShapeDtypeStruct(a.shape, a.dtype) for a in (gq, gk, gv, ig, wg)),
        in_specs=[vmem] * 5,
        out_specs=(anywhere,) * 5,
        scratch_shapes=[dma((5,))],
    )(*(pltpu.with_memory_space_constraint(a, pltpu.VMEM) for a in (gq, gk, gv, ig, wg)))
    return gq, gk, gv, ig, wg[None]


def solution(mesh):
    return jax.shard_map(
        per_device,
        mesh=mesh,
        in_specs=(
            P("seq", "exp"), P("seq", "exp"), P("seq", "exp"), P("seq", "exp"),
            P("seq", None), P("seq", None), P("seq", None), P("exp", None, None),
        ),
        out_specs=(
            P("seq", "exp"), P("seq", "exp"), P("seq", "exp"), P("seq", "exp"), P("exp", "seq", None),
        ),
        check_vma=False,
    )
```

```python
import jax
import jax.numpy as jnp
from jax import lax
from jax.experimental import pallas as pl
from jax.experimental.pallas import tpu as pltpu
from jax.sharding import PartitionSpec as P

MESH = pl.DeviceIdType.MESH
F32 = jnp.float32
BF16 = jnp.bfloat16
NX = 4
NY = 4
NZ = 8
NM = 2 * NY
DH = 128
HEADS = 4
TOK = 512
COL = 512
DIN = 1024
RB = 32
SHARE = 64


def mm(a, b, ca, cb):
    return lax.dot_general(a, b, (((ca,), (cb,)), ((), ())), preferred_element_type=F32)


def rcopy(src, dst, ssem, rsem, seq, exp):
    return pltpu.make_async_remote_copy(
        src_ref=src,
        dst_ref=dst,
        send_sem=ssem,
        recv_sem=rsem,
        device_id={"seq": seq, "exp": exp},
        device_id_type=MESH,
    )


def ring(count, place, neighbour, block, slots, ssem, rsem, drains):
    pairs = []
    for far in (True, False):
        hops = count // 2 if far else (count - 1) // 2
        pairs.append((hops, [(e, 1 if (e == 0) == far else -1) for e in range(2)]))
    drains.append((slots, ssem))

    def index(pair, hop):
        return hop + (0 if pair == 0 else pairs[0][0])

    def go(src, pair, i, hop):
        seq, exp = neighbour(pairs[pair][1][i][1])
        at = index(pair, hop)
        rcopy(src, slots.at[at, i], ssem, rsem.at[at], seq, exp).start()

    def arrived(pair, hop):
        seq, exp = neighbour(1)
        at = index(pair, hop)
        rcopy(slots.at[at], slots.at[at], ssem, rsem.at[at], seq, exp).wait_recv()

    for hop in range(count // 2):
        for pair, (hops, flows) in enumerate(pairs):
            if hop >= hops:
                continue
            if hop:
                arrived(pair, hop - 1)
            for i, (e, sign) in enumerate(flows):
                dest = lax.rem(place + sign * (hops - hop) + 2 * count, count)
                if hop:
                    ref = slots.at[index(pair, hop - 1), i]
                    ref[...] = (ref[...].astype(F32) + block(e, dest)[...].astype(F32)).astype(BF16)
                    go(ref, pair, i, hop)
                else:
                    go(block(e, dest), pair, i, 0)
            if not hop:
                yield None
        if hop:
            yield None
    for pair, (hops, _) in enumerate(pairs):
        arrived(pair, hops - 1)
    for e in range(2):
        total = block(e, place)[...].astype(F32)
        for pair, (hops, _) in enumerate(pairs):
            total = total + slots[index(pair, hops - 1), e].astype(F32)
        yield total


def step(generator, times=1):
    for _ in range(times):
        value = next(generator)
    return value


def kernel(
    q_in, k_in, v_in, do_in, inp_in, ids_in, gates_in, w_ref,
    gq_out, gk_out, gv_out, ig_out, wg_out,
    q_ref, k_ref, v_ref, do_ref, inp_ref, ids_ref, gates_ref,
    own_states, got_states, z_totals, z_own, back_states, states, base,
    intra, grads, other, gq_buf, in_own, in_other, rw_full, rw_own, rw_other,
    wy, wz, py, pz, y1, z2, z1, y2, xr, ry, rz, fin, wg_got, wg_buf,
    wx, relay, far_grads, ig_acc, ig_send, ig_buf,
    a_s, a_r, b_s, b_r, c_s, c_r, y1_s, y1_r, z2_s, z2_r, z1_s, z1_r, y2_s, y2_r, x_s, x_r,
    f_s, f_r, w_s, w_s2, w_r, h_s, h_r, k_s, k_r, p_s, p_r, loc, load,
):
    s = lax.axis_index("seq")
    x = lax.axis_index("exp")
    m = lax.rem(s, NM)
    z = s // NM
    c = lax.rem(s, 2)
    y = m // 2
    mate = s + 1 - 2 * c
    sends, drains = [], []
    most = pl.ds(0, NM - 1)

    def at_y(sign):
        return z * NM + lax.rem(y + sign + NY, NY) * 2 + c, x

    def at_z(sign):
        return lax.rem(z + sign + NZ, NZ) * NM + m, x

    def at_x(sign):
        return s, lax.rem(x + sign + NX, NX)

    barrier = pltpu.get_barrier_semaphore()
    peers = 0
    for d in range(1, NM):
        pl.semaphore_signal(barrier, inc=1, device_id={"seq": z * NM + lax.rem(m + d, NM), "exp": x}, device_id_type=MESH)
        peers += 1
    for d in range(1, NZ):
        pl.semaphore_signal(barrier, inc=1, device_id={"seq": lax.rem(z + d, NZ) * NM + m, "exp": x}, device_id_type=MESH)
        peers += 1
    for d in range(1, NX):
        for other_core in range(2):
            pl.semaphore_signal(barrier, inc=1, device_id={"seq": s - c + other_core, "exp": lax.rem(x + d, NX)}, device_id_type=MESH)
            peers += 1

    pairs = (
        (k_in, k_ref), (v_in, v_ref), (q_in, q_ref), (do_in, do_ref),
        (ids_in, ids_ref), (gates_in, gates_ref), (inp_in, inp_ref),
    )
    loads = [pltpu.make_async_copy(src, dst, load.at[i]) for i, (src, dst) in enumerate(pairs)]
    for copy in loads[:4]:
        copy.start()

    for copy in loads[:2]:
        copy.wait()

    def own_kv(h, _):
        cols = pl.ds(pl.multiple_of(h * DH, DH), DH)
        own_states[2 * h] = mm(k_ref[:, cols], v_ref[:, cols], 0, 0).astype(BF16)
        return 0

    lax.fori_loop(0, HEADS, own_kv, 0)
    for copy in loads[2:4]:
        copy.wait()
    for copy in loads[4:]:
        copy.start()

    def own_qo(h, _):
        cols = pl.ds(pl.multiple_of(h * DH, DH), DH)
        own_states[2 * h + 1] = mm(q_ref[:, cols], do_ref[:, cols], 0, 0).astype(BF16)
        return 0

    lax.fori_loop(0, HEADS, own_qo, 0)

    pl.semaphore_wait(barrier, peers)

    def part_of(u):
        return pl.ds(u * (DH // 2), DH // 2)

    for u in range(2):
        for d in range(1, NM):
            p = lax.rem(m + d, NM)
            rcopy(own_states.at[p, part_of(u)], got_states.at[m, part_of(u)], a_s, a_r.at[u], z * NM + p, x).start()
    got_states[m] = own_states[m]

    def w_cols(rows, part, xx):
        return w_ref.at[0, rows, pl.ds(pl.multiple_of(part * (NX * COL) + xx * COL, COL), COL)]

    start_row = c * (DIN // 2)
    half = pl.ds(pl.multiple_of(start_row, DIN // 2), DIN // 2)
    left, right = lax.rem(x + 3, NX), lax.rem(x + 1, NX)
    toward = lax.rem(x + 1 + 2 * c, NX)
    across = lax.rem(x + 2, NX)
    odd = lax.rem(z, 2)

    def w_rows(offset, count):
        return pl.ds(pl.multiple_of(start_row + offset, 16), count)

    alone = DIN // 2 - 4 * SHARE
    shared = w_rows(alone + 2 * SHARE * odd, 2 * SHARE)
    for rows, sem in ((shared, 0), (w_rows(0, alone), 1)):
        for to in (right, left):
            for part in range(2):
                rcopy(w_cols(rows, part, to), wx.at[x, rows, pl.ds(part * COL, COL)], w_s, w_r.at[sem], s, to).start()
    drains.append((wx.at[0, pl.ds(0, DIN - 4 * SHARE)], w_s))

    def share_weights():
        ref = wx.at[0, pl.ds(0, 4 * SHARE)]
        rcopy(ref, ref, w_s, w_r.at[0], s, toward).wait_recv()
        for e in (left, right):
            for i, sign in ((0, 1 - 2 * odd), (1, 2 * odd - 1)):
                ref = wx.at[e, w_rows(alone + 2 * SHARE * odd + SHARE * i, SHARE)]
                seq, exp = at_z(sign)
                rcopy(ref, ref, w_s2, w_r.at[2], seq, exp).start()
        drains.append((wx.at[0, pl.ds(0, 4 * SHARE)], w_s2))

    def all_weights():
        ref = wx.at[0, pl.ds(0, 2 * alone)]
        rcopy(ref, ref, w_s, w_r.at[1], s, toward).wait_recv()
        ref = wx.at[0, pl.ds(0, 4 * SHARE)]
        rcopy(ref, ref, w_s, w_r.at[2], s, toward).wait_recv()

    for copy in loads[4:]:
        copy.wait()
    lane = lax.broadcasted_iota(jnp.int32, (TOK, DH), 1)
    expert = lax.broadcasted_iota(jnp.int32, (DH, TOK), 0)
    rw = jnp.where(ids_ref[0:1, :] == expert, gates_ref[0:1, :], 0.0) + jnp.where(
        ids_ref[1:2, :] == expert, gates_ref[1:2, :], 0.0
    )
    rw_full[...] = rw.T
    rw_own[...] = rw[0:8, :]

    def turn(j, _):
        cols = pl.ds(pl.multiple_of(j * DH, DH), DH)
        in_own[cols, :] = inp_ref[:, cols].astype(F32).T.astype(BF16)
        return 0

    lax.fori_loop(0, DIN // DH, turn, 0)
    for i, (src, dst) in enumerate(((in_own, in_other), (rw_own, rw_other))):
        copy = rcopy(src, dst, p_s.at[i], p_r.at[i], mate, x)
        copy.start()
        sends.append(copy)

    own_w = [
        pltpu.make_async_copy(
            w_cols(pl.ds(0, DIN), part, xx), wx.at[slot, :, pl.ds(part * COL, COL)], loc.at[0]
        )
        for xx, slot in ((x, across), (across, x))
        for part in range(2)
    ]

    def inside(h, _):
        cols = pl.ds(pl.multiple_of(h * DH, DH), DH)
        qh, kh, vh, doh = q_ref[:, cols], k_ref[:, cols], v_ref[:, cols], do_ref[:, cols]
        row = lax.broadcasted_iota(jnp.int32, (TOK, TOK), 0)
        col = lax.broadcasted_iota(jnp.int32, (TOK, TOK), 1)
        first = jnp.where(row >= col, mm(doh, vh, 1, 1), 0.0).astype(BF16)
        intra[0, :, cols] = mm(first, kh, 1, 0)
        third = jnp.where(row <= col, mm(vh, doh, 1, 1), 0.0).astype(BF16)
        intra[1, :, cols] = mm(third, qh, 1, 0)
        middle = jnp.where(row <= col, mm(kh, qh, 1, 1), 0.0).astype(BF16)
        intra[2, :, cols] = mm(middle, doh, 1, 0)
        return 0

    lax.fori_loop(0, HEADS // 2, inside, 0)

    forward = c == 0
    drains.append((own_states.at[most], a_s))

    def sum_of(u):
        total = got_states[0, part_of(u), :].astype(F32)
        for p in range(1, NM):
            total = total + got_states[p, part_of(u), :].astype(F32)
        return total

    def step_b(u):
        ref = got_states.at[most, part_of(u)]
        rcopy(ref, ref, a_s, a_r.at[u], mate, x).wait_recv()
        z_own[part_of(u), :] = sum_of(u).astype(BF16)
        for d in range(1, NZ):

            @pl.when(forward == (z + d < NZ))
            def _():
                rcopy(
                    z_own.at[part_of(u)], z_totals.at[z, part_of(u)],
                    b_s.at[d], b_r.at[u, d], lax.rem(z + d, NZ) * NM + m, x,
                ).start()

    step_b(0)
    step_b(1)

    for copy in own_w:
        copy.start()
    lax.fori_loop(HEADS // 2, HEADS, inside, 0)

    def weigh(src, weights, lanes):
        def one(q, _):
            yy = lax.rem(q, NY)
            zz = q // NY
            block = src[pl.ds(pl.multiple_of(q * RB, RB), RB), :].astype(F32)
            for e in range(2):
                value = (block * weights[e : e + 1, :]).astype(BF16)
                wy[yy, pl.ds(pl.multiple_of(e * NZ * RB + zz * RB, RB), RB), lanes] = value
                value = (block * weights[2 + e : 3 + e, :]).astype(BF16)
                wz[zz, pl.ds(pl.multiple_of(e * NY * RB + yy * RB, RB), RB), lanes] = value
            return 0

        lax.fori_loop(0, NY * NZ, one, 0)

    weigh(in_own, rw_own, pl.ds(0, TOK))

    def step_c(u):
        rows = part_of(u)
        base[...] = jnp.zeros_like(base)
        for d in range(1, NZ):
            source = lax.rem(z + NZ - d, NZ)

            @pl.when(forward == (z >= d))
            def _():
                ref = z_totals.at[source, rows]
                rcopy(ref, ref, b_s.at[d], b_r.at[u, d], source * NM + m, x).wait_recv()
                base[...] += ref[...].astype(F32)

        start = base[...]
        before = jnp.zeros_like(start)
        total = sum_of(u)
        for p in range(NM):
            piece = got_states[p, rows, :].astype(F32)
            back_states[p, rows, :] = (start + jnp.where(forward, before, total - before - piece)).astype(BF16)
            before = before + piece
        for d in range(1, NM):
            p = lax.rem(m + d, NM)
            rcopy(back_states.at[p, rows], states.at[m, rows], c_s, c_r.at[u], z * NM + p, x).start()

    step_c(0)
    step_c(1)
    states[m] = back_states[m]
    share_weights()

    rcopy(in_own, in_other, p_s.at[0], p_r.at[0], mate, x).wait_recv()
    rcopy(rw_own, rw_other, p_s.at[1], p_r.at[1], mate, x).wait_recv()
    weigh(in_other, rw_other, pl.ds(TOK, TOK))

    for u in range(2):
        ref = states.at[most, part_of(u)]
        rcopy(ref, ref, c_s, c_r.at[u], mate, x).wait_recv()
    drains.append((back_states.at[most], c_s))

    for h in range(HEADS):
        cols = slice(h * DH, (h + 1) * DH)
        late = states[2 * h + 1]
        grads[0, :, cols] = (intra[1, :, cols] + mm(v_ref[:, cols], late, 1, 1)).astype(BF16)
        grads[1, :, cols] = (intra[2, :, cols] + mm(k_ref[:, cols], late, 1, 0)).astype(BF16)
    copy = rcopy(grads.at[1 - c], other, p_s.at[2], p_r.at[2], mate, x)
    copy.start()
    sends.append(copy)

    def tokens(part):
        return pl.ds(part * (TOK // 2), TOK // 2)

    for part in range(2):
        rcopy(grads.at[:, tokens(part)], relay.at[:, tokens(part)], k_s, k_r.at[0, part], s, toward).start()
    drains.append((wx.at[0], k_s))

    def pass_on(part):
        ref = relay.at[:, tokens(part)]
        rcopy(ref, ref, k_s, k_r.at[0, part], s, toward).wait_recv()
        rcopy(ref, far_grads.at[:, tokens(part)], k_s, k_r.at[1, part], s, toward).start()

    def scale_of(e, rows):
        return jnp.sum(jnp.where(lane[rows] == e, rw_full[rows, :], 0.0), axis=1, keepdims=True)

    def project(e, slot, fresh, first, last):
        scale = scale_of(e, slice(0, TOK))

        def one(j, _):
            rows = pl.ds(pl.multiple_of(j * (DIN // NX), DIN // NX), DIN // NX)
            value = mm(grads[0], wx[slot, rows, 0:COL], 1, 1) + mm(grads[1], wx[slot, rows, COL : 2 * COL], 1, 1)
            value = scale * value
            ig_acc[j] = value if fresh else ig_acc[j] + value
            return 0

        lax.fori_loop(first, last, one, 0)


    pltpu.make_async_copy(wx.at[pl.ds(0, 2)], wx.at[pl.ds(0, 2)], loc.at[0]).wait()
    project(x, across, True, 0, 2)
    rcopy(grads.at[0], other, p_s.at[2], p_r.at[2], mate, x).wait_recv()

    def dot_y(d, u):
        yy = lax.rem(y + d + NY, NY)
        cols = slice(u * (COL // 2), (u + 1) * (COL // 2))
        for part in range(2):
            rows = pl.ds(part * 256, 256)
            value = mm(wy[yy, rows, 0:TOK], grads[c, :, cols], 1, 0) + mm(wy[yy, rows, TOK : 2 * TOK], other[:, cols], 1, 0)
            py[u, yy, rows, :] = value.astype(BF16)

    def dot_z(d, u):
        zz = lax.rem(z + d + NZ, NZ)
        cols = slice(u * (COL // 2), (u + 1) * (COL // 2))
        value = mm(wz[zz, :, 0:TOK], grads[c, :, cols], 1, 0) + mm(wz[zz, :, TOK : 2 * TOK], other[:, cols], 1, 0)
        pz[u, zz] = value.astype(BF16)

    ring_y1 = [
        ring(NY, y, at_y, lambda e, d, u=u: py.at[u, d, pl.ds(e * NZ * RB, NZ * RB)], y1.at[u], y1_s.at[u], y1_r.at[u], drains)
        for u in range(2)
    ]
    ring_z1 = [
        ring(NZ, z, at_z, lambda e, d, u=u: pz.at[u, d, pl.ds(e * NY * RB, NY * RB)], z1.at[u], z1_s.at[u], z1_r.at[u], drains)
        for u in range(2)
    ]
    ring_z2 = ring(
        NZ, z, at_z,
        lambda e, d: ry.at[pl.ds(pl.multiple_of(e * NZ * RB + d * RB, RB), RB)],
        z2, z2_s, z2_r, drains,
    )
    ring_y2 = ring(
        NY, y, at_y,
        lambda e, d: rz.at[pl.ds(pl.multiple_of(e * NY * RB + d * RB, RB), RB)],
        y2, y2_s, y2_r, drains,
    )
    ring_x = [
        ring(
            NX, x, at_x,
            lambda e, d, u=u: ig_send.at[d, pl.ds(u * (TOK // 2) + e * (TOK // 4), TOK // 4)],
            xr.at[u], x_s.at[u], x_r.at[u], drains,
        )
        for u in range(2)
    ]

    def y1_done(u):
        for e in range(2):
            ry[pl.ds(e * NZ * RB, NZ * RB), pl.ds(u * (COL // 2), COL // 2)] = step(ring_y1[u]).astype(BF16)

    def z1_done(u):
        for e in range(2):
            rz[pl.ds(e * NY * RB, NY * RB), pl.ds(u * (COL // 2), COL // 2)] = step(ring_z1[u]).astype(BF16)

    def hand_over(way, e):
        ref = wx.at[e, half]
        rcopy(ref, ref, h_s, h_r.at[way], mate, x).start()

    drains.append((wx.at[0], h_s))

    def handed(way, e):
        ref = wx.at[e, pl.ds(pl.multiple_of((1 - c) * (DIN // 2), DIN // 2), DIN // 2)]
        rcopy(ref, ref, h_s, h_r.at[way], mate, x).wait_recv()

    def last_project(u):
        ref = far_grads.at[:, tokens(u)]
        rcopy(ref, ref, k_s, k_r.at[1, u], s, toward).wait_recv()
        scale = scale_of(x, slice(u * (TOK // 2), (u + 1) * (TOK // 2)))

        def one(j, _):
            rows = pl.ds(pl.multiple_of(j * (DIN // NX), DIN // NX), DIN // NX)
            value = mm(far_grads[0, tokens(u), :], wx[x, rows, 0:COL], 1, 1) + mm(
                far_grads[1, tokens(u), :], wx[x, rows, COL : 2 * COL], 1, 1
            )
            ig_send[j, tokens(u), :] = (ig_acc[j, tokens(u), :] + scale * value).astype(BF16)
            return 0

        lax.fori_loop(0, NX, one, 0)
        step(ring_x[u], 2)

    def finish(e, total):
        fin[e] = total.astype(BF16)
        for core in range(2):
            src = fin.at[e, pl.ds(core * (RB // 2), RB // 2)]
            dst = wg_got.at[:, pl.ds(pl.multiple_of(c * (NX * COL) + x * COL, COL), COL)]
            here = jnp.logical_and(x == e, c == core)

            @pl.when(jnp.logical_not(here))
            def _():
                rcopy(src, dst, f_s, f_r, s - c + core, e).start()

            @pl.when(here)
            def _():
                dst[...] = src[...]

    def finish_y():
        for e in range(2):
            finish(2 + e, step(ring_y2))

    def finish_z():
        for e in range(2):
            finish(e, step(ring_z2))

    def ig_done(u):
        for e in range(2):
            ig_buf[pl.ds(u * (TOK // 2) + e * (TOK // 4), TOK // 4), :] = step(ring_x[u]).astype(BF16)

    dot_y(2, 0)
    step(ring_y1[0])
    dot_z(4, 0)
    step(ring_z1[0])
    dot_z(4, 1)
    step(ring_z1[1])
    dot_y(1, 0)
    dot_y(-1, 0)
    step(ring_y1[0])
    for u in range(2):
        dot_z(3, u)
        dot_z(-3, u)
        step(ring_z1[u])
    for h in range(HEADS):
        cols = slice(h * DH, (h + 1) * DH)
        gq_buf[:, cols] = (intra[0, :, cols] + mm(do_ref[:, cols], states[2 * h], 1, 1)).astype(BF16)
    outs = [
        pltpu.make_async_copy(gq_buf, gq_out, loc.at[1]),
        pltpu.make_async_copy(grads.at[0], gk_out, loc.at[2]),
        pltpu.make_async_copy(grads.at[1], gv_out, loc.at[3]),
    ]
    for copy in outs:
        copy.start()
    all_weights()
    hand_over(0, left)
    hand_over(1, right)
    dot_y(2, 1)
    dot_y(1, 1)
    dot_y(-1, 1)
    dot_z(2, 0)
    dot_z(-2, 0)
    step(ring_y1[0])
    step(ring_y1[1], 2)
    dot_z(2, 1)
    dot_z(-2, 1)
    dot_y(0, 0)
    step(ring_z1[0])
    project(x, across, True, 2, 4)
    step(ring_z1[1])
    pass_on(0)
    dot_y(0, 1)
    for d in (1, -1, 0):
        dot_z(d, 0)
        dot_z(d, 1)
    handed(0, left)
    project(left, left, False, 0, 2)
    step(ring_z1[0])
    project(left, left, False, 2, 4)
    step(ring_y1[1])
    pass_on(1)
    step(ring_z1[1])
    handed(1, right)
    project(right, right, False, 0, 2)
    step(ring_z1[0])
    y1_done(0)
    project(right, right, False, 2, 4)
    step(ring_z1[1])
    y1_done(1)
    step(ring_z2, 2)
    last_project(0)
    z1_done(0)
    step(ring_z2)
    z1_done(1)
    step(ring_y2, 2)
    step(ring_z2)
    last_project(1)
    step(ring_y2)
    step(ring_x[0])
    step(ring_z2)
    finish_y()
    finish_z()
    step(ring_x[1])
    ig_done(0)
    arriving = wg_got.at[:, pl.ds(0, (2 * NX - 1) * COL)]
    rcopy(arriving, arriving, f_s, f_r, mate, x).wait_recv()
    drains.append((arriving, f_s))
    wg_buf[...] = wg_got[...].astype(F32)
    outs.append(pltpu.make_async_copy(wg_buf, wg_out, loc.at[4]))
    outs[-1].start()
    ig_done(1)
    outs.append(pltpu.make_async_copy(ig_buf, ig_out, loc.at[5]))
    outs[-1].start()

    for copy in sends:
        copy.wait_send()
    for d in range(1, NZ):

        @pl.when(forward == (z + d < NZ))
        def _():
            rcopy(z_own, z_own, b_s.at[d], b_r.at[0, d], mate, x).wait_send()

    for ref, sem in drains:
        rcopy(ref, ref, sem, a_r.at[0], mate, x).wait_send()
    for copy in outs:
        copy.wait()


def write_out(*refs):
    sems = refs[10]
    copies = [pltpu.make_async_copy(refs[i], refs[5 + i], sems.at[i]) for i in range(5)]
    for copy in copies:
        copy.start()
    for copy in copies:
        copy.wait()


def per_device(query_in, key_in, value_in, out_grad, inputs, expert_ids, route_gates, expert_weight):
    vmem = pl.BlockSpec(memory_space=pltpu.VMEM)
    anywhere = pl.BlockSpec(memory_space=pl.ANY)
    dma = pltpu.SemaphoreType.DMA

    def v(shape, dtype=BF16):
        return pltpu.VMEM(shape, dtype)

    scratch = [
        v((TOK, COL)), v((TOK, COL)), v((TOK, COL)), v((TOK, COL)), v((TOK, DIN)), v((2, TOK), jnp.int32), v((2, TOK), F32),
        v((NM, DH, DH)), v((NM, DH, DH)), v((NZ, DH, DH)), v((DH, DH)), v((NM, DH, DH)), v((NM, DH, DH)),
        v((DH // 2, DH), F32),
        v((3, TOK, COL), F32), v((2, TOK, COL)), v((TOK, COL)), v((TOK, COL)),
        v((DIN, TOK)), v((DIN, TOK)), v((TOK, DH), F32), v((8, TOK), F32), v((8, TOK), F32),
        v((NY, 2 * NZ * RB, 2 * TOK)), v((NZ, 2 * NY * RB, 2 * TOK)),
        v((2, NY, 2 * NZ * RB, COL // 2)), v((2, NZ, 2 * NY * RB, COL // 2)),
        v((2, NY - 1, 2, NZ * RB, COL // 2)), v((NZ - 1, 2, RB, COL)),
        v((2, NZ - 1, 2, NY * RB, COL // 2)), v((NY - 1, 2, RB, COL)),
        v((2, NX - 1, 2, TOK // 4, DIN // NX)),
        v((2 * NZ * RB, COL)), v((2 * NY * RB, COL)),
        v((NX, RB, COL)), v((RB // 2, 2 * NX * COL)), v((RB // 2, 2 * NX * COL), F32),
        v((NX, DIN, 2 * COL)), v((2, TOK, COL)), v((2, TOK, COL)),
        v((NX, TOK, DIN // NX), F32), v((NX, TOK, DIN // NX)), v((TOK, DIN // NX)),
        dma(()), dma((2,)), dma((NZ,)), dma((2, NZ)), dma(()), dma((2,)),
        dma((2,)), dma((2, NY - 1)), dma(()), dma((NZ - 1,)),
        dma((2,)), dma((2, NZ - 1)), dma(()), dma((NY - 1,)),
        dma((2,)), dma((2, NX - 1)),
        dma(()), dma(()), dma(()), dma(()), dma((3,)), dma(()), dma((2,)),
        dma(()), dma((2, 2)), dma((3,)), dma((3,)), dma((6,)), dma((7,)),
    ]
    gq, gk, gv, ig, wg = pl.pallas_call(
        kernel,
        out_shape=(
            pltpu.VMEM((TOK, COL), BF16),
            pltpu.VMEM((TOK, COL), BF16),
            pltpu.VMEM((TOK, COL), BF16),
            pltpu.VMEM((TOK, DIN // NX), BF16),
            pltpu.VMEM((RB // 2, 2 * NX * COL), F32),
        ),
        in_specs=[anywhere] * 8,
        out_specs=(anywhere,) * 5,
        scratch_shapes=scratch,
        compiler_params=pltpu.CompilerParams(
            collective_id=0, has_side_effects=True, vmem_limit_bytes=56 * 1024 * 1024
        ),
    )(query_in, key_in, value_in, out_grad, inputs, expert_ids.T, route_gates.T, expert_weight)
    gq, gk, gv, ig, wg = pl.pallas_call(
        write_out,
        out_shape=tuple(jax.ShapeDtypeStruct(a.shape, a.dtype) for a in (gq, gk, gv, ig, wg)),
        in_specs=[vmem] * 5,
        out_specs=(anywhere,) * 5,
        scratch_shapes=[dma((5,))],
    )(*(pltpu.with_memory_space_constraint(a, pltpu.VMEM) for a in (gq, gk, gv, ig, wg)))
    return gq, gk, gv, ig, wg[None]


def solution(mesh):
    return jax.shard_map(
        per_device,
        mesh=mesh,
        in_specs=(
            P("seq", "exp"), P("seq", "exp"), P("seq", "exp"), P("seq", "exp"),
            P("seq", None), P("seq", None), P("seq", None), P("exp", None, None),
        ),
        out_specs=(
            P("seq", "exp"), P("seq", "exp"), P("seq", "exp"), P("seq", "exp"), P("exp", "seq", None),
        ),
        check_vma=False,
    )
```
